32 devices in a mesh: grp: 1, row: 32 (over z, y, x, core).
Axes of the slice: x: 2, y: 2, z: 4, core: 2. Of those that a mesh axis runs over, the one named last changes fastest.
Arguments:
- features: bfloat16 [64, 192, 2048], P(('grp', 'row')), may hold values from -6 to 6
- branch_kernel_weight: bfloat16 [2048, 10, 128], P('row'), may hold values from -0.046875 to 0.046875
- branch_norm_bias: float32 [2, 128], replicated, may hold values from -3 to 3
- merge_weight: bfloat16 [256, 256], P('row'), may hold values from -0.375 to 0.375
- merge_bias: float32 [256], replicated, may hold values from -3 to 3
- cotangent: bfloat16 [64, 192, 256], P(('grp', 'row')), may hold values from -24 to 24
Outputs:
- merged: bfloat16 [64, 192, 256], P(('grp', 'row'))
- input_grad: bfloat16 [64, 192, 2048], P(('grp', 'row'))
- branch_kernel_gradient: float32 [2048, 10, 128], P(('grp', 'row'))
- grad_merge: float32 [256, 256], P(('grp', 'row'))
The draws below stay inside these ranges and needn't reach their ends.
All inputs are finite; a program needn't handle non-finite values.
Results may differ from the reference program's by a relative error of at most 0.023.
The reference program's roundings to bfloat16 on the way count: a program that leaves them out, or rounds other values in their place, can miss the bound.
Values may be sent and summed in bfloat16 or wider, within the bound.
No kernel may reach another device: no remote copies, remote signals or barrier semaphores. Data moves between devices by JAX's collectives and lax.ppermute only.
A program may use at most 128 MiB of HBM per device.

```python
import math
import jax
import jax.numpy as jnp
from jax import lax

INPUT_CHANNELS = 2048
BRANCH_CHANNELS = 128
FO = 256
DILATION_RATE = 18
MAP_COLUMNS = 192
H = 64


def strengthened(result, rng, source, target, blocks, factor):
    owner, partner = [(jnp.arange(result.shape[axis_at]) // (result.shape[axis_at] // blocks)).reshape([-1 if axis == axis_at else 1 for axis in range(result.ndim)]) for axis_at in (source, target)]
    chosen = jax.random.permutation(rng, blocks)[partner]
    strong = (owner == chosen) | (owner == (partner + blocks // 2) % blocks)
    return jnp.where(strong, factor * result, result)


def level_of(stream_key, dims, split, low, high):
    factor_of, own = 1.0, jax.random.fold_in(stream_key, 6)
    for axis_at, parts in split:
        steps = jnp.exp(jax.random.uniform(jax.random.fold_in(own, axis_at), (parts,), jnp.float32, low / len(split), high / len(split)))
        factor_of = factor_of * jnp.repeat(steps, dims[axis_at] // parts).reshape([-1 if axis == axis_at else 1 for axis in range(len(dims))])
    return factor_of


def centred(stream_key, dims, scale, limit, split=(), kind=jnp.bfloat16):
    values = jax.random.normal(stream_key, dims, jnp.float32) * scale
    if len(split) > 0:
        values = level_of(stream_key, dims, split, -0.22, 0.18) * values
    return jnp.clip(values, min=-limit, max=limit).astype(kind)


def bell_draw_with(key, extent, scale, most, cuts, heavy, dtype=jnp.bfloat16):
    entries = scale * jax.random.normal(key, extent, jnp.float32)
    if cuts:
        entries = entries * level_of(key, extent, cuts, -0.22, 0.18)
    return jnp.clip(strengthened(entries, jax.random.fold_in(key, 3), *heavy), -most, most).astype(dtype)


def setup_inputs(seed: int = 0, part: int = 0) -> dict:
    keys = jax.random.split(jax.random.key(seed), 7)
    part_keys = jax.random.split(jax.random.fold_in(keys[6], part), 7)
    return {
        "features": bell_draw_with(part_keys[0], (H, MAP_COLUMNS, INPUT_CHANNELS), 1.0, 6.0, ((0, 32),), (0, 2, 32, 2.75)),
        "branch_kernel_weight": centred(keys[1], (INPUT_CHANNELS, 10, BRANCH_CHANNELS), (9 * INPUT_CHANNELS) ** -0.5, 0.046875, ((0, 32),)),
        "branch_norm_bias": centred(keys[2], (2, BRANCH_CHANNELS), 0.5, 3.0, (), jnp.float32),
        "merge_weight": centred(keys[3], (2 * BRANCH_CHANNELS, FO), (2 * BRANCH_CHANNELS) ** -0.5, 0.375, ((0, 32),)),
        "merge_bias": centred(keys[4], (FO,), 0.5, 3.0, (), jnp.float32),
        "cotangent": centred(part_keys[5], (H, MAP_COLUMNS, FO), 4.0, 24.0, ((0, 32),)),
    }


def transposed_product(left, right):
    return lax.dot_general(left, right, (((0,), (0,)), ((), ())), preferred_element_type=jnp.float32)

def ndot(left, right):
    return lax.dot_general(left, right, (((1,), (1,)), ((), ())), preferred_element_type=jnp.float32)

def reference(features, branch_kernel_weight, branch_norm_bias, merge_weight, merge_bias, cotangent):
    map_height = features.shape[0]
    pixel_count = map_height * MAP_COLUMNS
    flattened = features.reshape(pixel_count, INPUT_CHANNELS)
    padded_input = jnp.pad(features, ((DILATION_RATE, DILATION_RATE), (DILATION_RATE, DILATION_RATE), (0, 0)))

    def window(tap_number):
        tap_row_index = tap_number // 3
        tap_column = tap_number % 3
        return padded_input[tap_row_index * DILATION_RATE:tap_row_index * DILATION_RATE + map_height, tap_column * DILATION_RATE:tap_column * DILATION_RATE + MAP_COLUMNS].reshape(pixel_count, INPUT_CHANNELS)
    z_one = jnp.dot(flattened, branch_kernel_weight[:, 0, :], preferred_element_type=jnp.float32)
    dilated_preactivation = jnp.zeros((pixel_count, BRANCH_CHANNELS), jnp.float32)
    for tap_number in range(9):
        dilated_preactivation = dilated_preactivation + jnp.dot(window(tap_number), branch_kernel_weight[:, 1 + tap_number, :], preferred_element_type=jnp.float32)
    pointwise_activation = jnp.maximum(z_one + branch_norm_bias[0], 0.0).astype(jnp.bfloat16)
    dilated_activation = jnp.maximum(dilated_preactivation + branch_norm_bias[1], 0.0).astype(jnp.bfloat16)
    combined = jnp.concatenate([pointwise_activation, dilated_activation], axis=1)
    merged = jnp.maximum(jnp.dot(combined, merge_weight, preferred_element_type=jnp.float32) + merge_bias, 0.0).astype(jnp.bfloat16)
    grad_out = jnp.where(merged > 0, cotangent.reshape(pixel_count, FO), jnp.zeros((), jnp.bfloat16))
    gradient_scale = 1.0 / math.sqrt(pixel_count)
    grad_merge = transposed_product(combined, grad_out) * gradient_scale
    backward_pass = ndot(grad_out, merge_weight)
    pointwise_gradient = jnp.where(pointwise_activation > 0, backward_pass[:, :BRANCH_CHANNELS], 0.0).astype(jnp.bfloat16)
    dilated_gradient = jnp.where(dilated_activation > 0, backward_pass[:, BRANCH_CHANNELS:], 0.0).astype(jnp.bfloat16)
    branch_kernel_gradient = jnp.stack([transposed_product(flattened, pointwise_gradient)] + [transposed_product(window(tap_number), dilated_gradient) for tap_number in range(9)], axis=1) * gradient_scale
    gradient_padding = jnp.pad(dilated_gradient.reshape(map_height, MAP_COLUMNS, BRANCH_CHANNELS), ((DILATION_RATE, DILATION_RATE), (DILATION_RATE, DILATION_RATE), (0, 0)))
    input_grad = ndot(pointwise_gradient, branch_kernel_weight[:, 0, :])
    for tap_number in range(9):
        tap_row_index = tap_number // 3
        tap_column = tap_number % 3
        shifted = gradient_padding[(2 - tap_row_index) * DILATION_RATE:(2 - tap_row_index) * DILATION_RATE + map_height, (2 - tap_column) * DILATION_RATE:(2 - tap_column) * DILATION_RATE + MAP_COLUMNS].reshape(pixel_count, BRANCH_CHANNELS)
        input_grad = input_grad + ndot(shifted, branch_kernel_weight[:, 1 + tap_number, :])
    return (merged.reshape(map_height, MAP_COLUMNS, FO), input_grad.astype(jnp.bfloat16).reshape(map_height, MAP_COLUMNS, INPUT_CHANNELS), branch_kernel_gradient, grad_merge)
```

```python
import math

import jax
import jax.numpy as jnp
from jax import lax
from jax.sharding import PartitionSpec as P

DILATION_RATE = 18
PORTIONS = ((1, 2, 3), (7, 8, 9), (0, 4, 5, 6))


def passed_along(block, distance):
    devices = range(lax.axis_size("row"))
    route = [(i - distance, i) for i in devices if i - distance in devices]
    return lax.ppermute(block, "row", route)


def exchanged(block, bit):
    return lax.ppermute(block, "row", [(i, i ^ (1 << bit)) for i in range(lax.axis_size("row"))])


def dot_f32(left, right, left_dim, right_dim):
    return lax.dot_general(
        left, right, (((left_dim,), (right_dim,)), ((), ())), preferred_element_type=jnp.float32
    )


def bit_orders(bit_count):
    far = list(range(bit_count - 1, 3, -1))
    near = [b for b in (3, 2, 1) if b < bit_count]
    return [far + near[k:] + near[:k] for k in range(3)]


def axis_of(bit, bit_count):
    return 0 if bit == 0 else bit_count - bit


def gather_blocks(blocks, orders, bit_count):
    for step in range(bit_count):
        arrived = [exchanged(b, o[step]) for b, o in zip(blocks, orders)]
        blocks = [
            jnp.concatenate([b, a], axis=axis_of(o[step], bit_count))
            for b, a, o in zip(blocks, arrived, orders)
        ]
    return blocks


def scatter_block(block, order, bit_count, dtype):
    for bit in order:
        axis = axis_of(bit, bit_count)
        own = lax.slice_in_dim(block, 0, 1, axis=axis)
        other = lax.slice_in_dim(block, 1, 2, axis=axis).astype(dtype)
        block = own + exchanged(other, bit).astype(jnp.float32)
    return block


def relative_order(size, device_count, me):
    width = size // device_count
    target = lax.broadcasted_iota(jnp.int32, (size, size), 1)
    source = lax.broadcasted_iota(jnp.int32, (size, size), 0)
    half = device_count // 2
    block, inner = target // width, target % width
    device = (block % half) * 2 + block // half
    return (source == (device ^ me) * width + inner).astype(jnp.bfloat16)


def column_shifted(rows, shift):
    width = rows.shape[1]
    if shift == 0:
        return rows
    if shift > 0:
        return jnp.pad(rows[:, shift:], ((0, 0), (0, shift), (0, 0)))
    return jnp.pad(rows[:, : width + shift], ((0, 0), (-shift, 0), (0, 0)))


def on_device(
    features, branch_kernel_weight, branch_norm_bias, merge_weight, merge_bias, cotangent
):
    device_count = lax.axis_size("row")
    bit_count = device_count.bit_length() - 1
    me = lax.axis_index("row")
    rows, width, channels = features.shape
    taps, branch = branch_kernel_weight.shape[1:]
    own_channels = branch_kernel_weight.shape[0]
    joined_rows, merged_width = merge_weight.shape
    joined_width = joined_rows * device_count
    pixels = rows * width
    scale = 1.0 / math.sqrt(rows * device_count * width)
    device_step = DILATION_RATE // rows
    bits = (1,) * bit_count
    orders = [o + [0] for o in bit_orders(bit_count)]

    weight = branch_kernel_weight.transpose(1, 0, 2)
    blocks = [
        jnp.concatenate([weight[k] for k in portion], axis=1).reshape(bits + (own_channels, -1))
        for portion in PORTIONS
    ]
    blocks = gather_blocks(blocks, orders, bit_count)
    whole = [b.reshape(channels, b.shape[-1]) for b in blocks]
    (merge_block,) = gather_blocks(
        [merge_weight.reshape(bits + merge_weight.shape)], [list(range(bit_count))], bit_count
    )

    to_relative = relative_order(channels, device_count, me)
    flat = dot_f32(features.reshape(pixels, channels), to_relative, 1, 0).astype(jnp.bfloat16)
    merge_to_relative = relative_order(joined_width, device_count, me)
    whole_merge = dot_f32(
        merge_to_relative, merge_block.reshape(joined_width, merged_width), 1, 0
    ).astype(jnp.bfloat16)

    products = [dot_f32(flat, w, 1, 0) for w in whole]

    def row_sum(parts):
        total = None
        for j, part in enumerate(parts):
            moved = column_shifted(part.reshape(rows, width, branch), (j - 1) * DILATION_RATE)
            total = moved if total is None else total + moved
        return total

    def split(product):
        return [product[:, i * branch : (i + 1) * branch] for i in range(product.shape[1] // branch)]

    above = passed_along(row_sum(split(products[0])), device_step)
    below = passed_along(row_sum(split(products[1])), -device_step)
    centre = split(products[2])
    z_dil = (row_sum(centre[1:]) + above + below).reshape(pixels, branch)
    act_one = jnp.maximum(centre[0] + branch_norm_bias[0], 0.0).astype(jnp.bfloat16)
    act_dil = jnp.maximum(z_dil + branch_norm_bias[1], 0.0).astype(jnp.bfloat16)
    joined = jnp.concatenate([act_one, act_dil], axis=1)
    merged = jnp.maximum(dot_f32(joined, whole_merge, 1, 0) + merge_bias, 0.0).astype(jnp.bfloat16)
    grad_out = jnp.where(
        merged > 0, cotangent.reshape(pixels, merged_width), jnp.zeros((), jnp.bfloat16)
    )
    back = dot_f32(grad_out, whole_merge, 1, 1)
    grad_one = jnp.where(act_one > 0, back[:, :branch], 0.0).astype(jnp.bfloat16)
    grad_dil = jnp.where(act_dil > 0, back[:, branch:], 0.0).astype(jnp.bfloat16)
    grad_map = grad_dil.reshape(rows, width, branch)
    grad_rows = [passed_along(grad_map, -device_step), passed_along(grad_map, device_step), grad_map]

    def shifted_gradients(block):
        return [
            column_shifted(block, (1 - j) * DILATION_RATE).reshape(pixels, branch) for j in range(3)
        ]

    gradients = [
        jnp.concatenate(shifted_gradients(grad_rows[0]), axis=1),
        jnp.concatenate(shifted_gradients(grad_rows[1]), axis=1),
        jnp.concatenate([grad_one] + shifted_gradients(grad_rows[2]), axis=1),
    ]

    joined_relative = dot_f32(joined, merge_to_relative, 1, 0).astype(jnp.bfloat16)
    grad_merge = scatter_block(
        dot_f32(joined_relative, grad_out, 0, 0).reshape(
            (2,) * bit_count + (joined_rows, merged_width)
        ),
        list(range(bit_count)),
        bit_count,
        jnp.float32,
    ).reshape(joined_rows, merged_width) * scale

    weight_gradient = [None] * taps
    for portion, gradient, order in list(zip(PORTIONS, gradients, orders))[::-1]:
        total = dot_f32(flat, gradient, 0, 0).reshape(
            (2,) * bit_count + (own_channels, gradient.shape[1])
        )
        own = scatter_block(total, order[::-1], bit_count, jnp.bfloat16).reshape(own_channels, -1)
        for k, part in zip(portion, split(own)):
            weight_gradient[k] = part
    branch_kernel_gradient = jnp.stack(weight_gradient, axis=1) * scale

    input_total = sum(dot_f32(g, w, 1, 1) for g, w in zip(gradients, whole)).astype(jnp.bfloat16)
    input_grad = dot_f32(input_total, to_relative, 1, 1).astype(jnp.bfloat16)
    return (
        merged.reshape(rows, width, merged_width),
        input_grad.reshape(rows, width, channels),
        branch_kernel_gradient,
        grad_merge,
    )


def solution(mesh):
    placed = (
        P(("grp", "row"), None, None),
        P("row", None, None),
        P(),
        P("row", None),
        P(),
        P(("grp", "row"), None, None),
    )
    return jax.shard_map(
        on_device,
        mesh=mesh,
        in_specs=placed,
        out_specs=(
            P(("grp", "row"), None, None),
            P(("grp", "row"), None, None),
            P(("grp", "row"), None, None),
            P(("grp", "row"), None),
        ),
        check_vma=False,
    )
```

```python
import functools
import math

import jax
import jax.numpy as jnp
from jax import lax
from jax.experimental import pallas as pl
from jax.experimental.pallas import tpu as pltpu
from jax.sharding import PartitionSpec as P

DILATION_RATE = 18
LANES = 128
PORTIONS = ((1, 2, 3), (7, 8, 9), (0, 4, 5, 6))


def passed_along(block, distance):
    devices = range(lax.axis_size("row"))
    route = [(i - distance, i) for i in devices if i - distance in devices]
    return lax.ppermute(block, "row", route)


def exchanged(block, bit):
    return lax.ppermute(block, "row", [(i, i ^ (1 << bit)) for i in range(lax.axis_size("row"))])


def dot_f32(left, right, left_dim, right_dim):
    return lax.dot_general(
        left, right, (((left_dim,), (right_dim,)), ((), ())), preferred_element_type=jnp.float32
    )


def bit_orders(bit_count):
    near = [b for b in (3, 2, 1) if b < bit_count]
    return [near[k:] + near[:k] for k in range(3)]


def axis_of(bit, bit_count):
    return bit_count - 1 - bit


def after(value, *others):
    return lax.optimization_barrier((value,) + others)[0]


def together(*values):
    return list(lax.optimization_barrier(values))


def gathered(blocks, crossed, bit_count):
    arrived = together(*[exchanged(b, bit) for b, bit in zip(blocks, crossed)])
    return [
        jnp.concatenate([b, a], axis=axis_of(bit, bit_count))
        for b, a, bit in zip(blocks, arrived, crossed)
    ]


def added(own, arrived, bit, bit_count):
    axis = axis_of(bit, bit_count)

    def half(k):
        parts = [lax.slice_in_dim(x, k, k + 1, axis=axis) for x in (own, arrived)]
        return parts[0] + parts[1].astype(jnp.float32)

    return half(0), half(1).astype(jnp.bfloat16)


def halves(block, bit, bit_count):
    axis = axis_of(bit, bit_count)
    return (
        lax.slice_in_dim(block, 0, 1, axis=axis),
        lax.slice_in_dim(block, 1, 2, axis=axis).astype(jnp.bfloat16),
    )


def relative_order(size, device_count, me):
    width = size // device_count
    target = lax.broadcasted_iota(jnp.int32, (size, size), 1)
    source = lax.broadcasted_iota(jnp.int32, (size, size), 0)
    half = device_count // 2
    block, inner = target // width, target % width
    device = (block % half) * 2 + block // half
    return (source == (device ^ me) * width + inner).astype(jnp.bfloat16)


def reorder_kernel(me_ref, x_ref, own_ref, other_ref):
    me = me_ref[0]
    chip, core = me // 2, me % 2
    lane = lax.broadcasted_iota(jnp.int32, (x_ref.shape[0], LANES), 1)
    low_lane = lane < LANES // 2

    def tile(block):
        start = pl.multiple_of((block ^ chip) * LANES, LANES)
        return x_ref[:, pl.ds(start, LANES)].astype(jnp.float32)

    for t in range(own_ref.shape[1] // LANES):
        first, second = tile(2 * t), tile(2 * t + 1)
        low = jnp.where(low_lane, first, pltpu.roll(second, LANES // 2, 1)).astype(jnp.bfloat16)
        high = jnp.where(low_lane, pltpu.roll(first, LANES // 2, 1), second).astype(jnp.bfloat16)
        columns = slice(t * LANES, (t + 1) * LANES)
        own_ref[:, columns] = jnp.where(core == 0, low, high)
        other_ref[:, columns] = jnp.where(core == 0, high, low)


def reordered(flat, me):
    pixels, channels = flat.shape
    half = jax.ShapeDtypeStruct((pixels, channels // 2), flat.dtype)
    return pl.pallas_call(
        reorder_kernel,
        out_shape=(half, half),
        in_specs=[
            pl.BlockSpec(memory_space=pltpu.SMEM),
            pl.BlockSpec(memory_space=pltpu.VMEM),
        ],
        out_specs=(pl.BlockSpec(memory_space=pltpu.VMEM),) * 2,
        cost_estimate=pl.CostEstimate(
            flops=8 * pixels * channels, bytes_accessed=4 * pixels * channels, transcendentals=0
        ),
        name="reorder",
    )(me.reshape(1), flat)


def kernel_rows_kernel(order, w_ref, out_ref):
    for place, k in enumerate(order):
        out_ref[:, place * LANES : (place + 1) * LANES] = w_ref[k]


def kernel_rows(weight, order):
    taps, rows, branch = weight.shape
    return pl.pallas_call(
        functools.partial(kernel_rows_kernel, order),
        out_shape=jax.ShapeDtypeStruct((rows, taps * branch), weight.dtype),
        in_specs=[pl.BlockSpec(memory_space=pltpu.VMEM)],
        out_specs=pl.BlockSpec(memory_space=pltpu.VMEM),
        cost_estimate=pl.CostEstimate(flops=0, bytes_accessed=4 * weight.size, transcendentals=0),
        name="kernel_rows",
    )(weight)


def input_gradient_kernel(portion_count, me_ref, *refs):
    core = me_ref[0] % 2
    out_ref = refs[-1]
    total = None
    for p in range(portion_count):
        gradient_ref = refs[p]
        first = portion_count + 4 * p
        rows = []
        for k in range(2):
            own, other = refs[first + 2 * k][...], refs[first + 2 * k + 1][...]
            rows += [jnp.where(core == 0, own, other), jnp.where(core == 0, other, own)]
        part = dot_f32(gradient_ref[...], jnp.concatenate(rows, axis=0), 1, 1)
        total = part if total is None else total + part
    out_ref[...] = total.astype(out_ref.dtype)


def input_gradient(gradients, own, other, me):
    pixels = gradients[0].shape[0]
    half = own[0].shape[0]
    rows = LANES // 2
    operands, specs = list(gradients), [
        pl.BlockSpec(g.shape, lambda t, me_ref: (0, 0)) for g in gradients
    ]
    for a, b in zip(own, other):
        for k in range(2):
            for w in (a, b):
                operands.append(w)
                specs.append(
                    pl.BlockSpec(
                        (rows, w.shape[1]),
                        lambda t, me_ref, k=k: ((2 * t + k) ^ (me_ref[0] // 2), 0),
                    )
                )
    columns = sum(g.shape[1] for g in gradients)
    return pl.pallas_call(
        functools.partial(input_gradient_kernel, len(gradients)),
        out_shape=jax.ShapeDtypeStruct((pixels, 2 * half), jnp.bfloat16),
        grid_spec=pltpu.PrefetchScalarGridSpec(
            num_scalar_prefetch=1,
            grid=(half // LANES,),
            in_specs=specs,
            out_specs=pl.BlockSpec((pixels, 2 * LANES), lambda t, me_ref: (0, t)),
        ),
        cost_estimate=pl.CostEstimate(
            flops=4 * pixels * columns * half,
            bytes_accessed=2 * (pixels * columns + 2 * half * columns + 2 * pixels * half),
            transcendentals=0,
        ),
        name="input_gradient",
    )(me.reshape(1), *operands)


def column_shifted(rows, shift):
    width = rows.shape[1]
    if shift == 0:
        return rows
    if shift > 0:
        return jnp.pad(rows[:, shift:], ((0, 0), (0, shift), (0, 0)))
    return jnp.pad(rows[:, : width + shift], ((0, 0), (-shift, 0), (0, 0)))


def on_device(
    features, branch_kernel_weight, branch_norm_bias, merge_weight, merge_bias, cotangent
):
    device_count = lax.axis_size("row")
    bit_count = device_count.bit_length() - 1
    me = lax.axis_index("row")
    rows, width, channels = features.shape
    taps, branch = branch_kernel_weight.shape[1:]
    own_channels = branch_kernel_weight.shape[0]
    joined_rows, merged_width = merge_weight.shape
    joined_width = joined_rows * device_count
    pixels = rows * width
    scale = 1.0 / math.sqrt(rows * device_count * width)
    device_step = DILATION_RATE // rows
    bits = (1,) * (bit_count - 1)
    orders = bit_orders(bit_count)
    far_bits = list(range(bit_count - 1, 3, -1))
    paired = 2 * own_channels == LANES
    portion_widths = [len(p) * branch for p in PORTIONS]

    def split(array, widths):
        starts = [sum(widths[:i]) for i in range(len(widths))]
        return [lax.slice_in_dim(array, s, s + w, axis=-1) for s, w in zip(starts, widths)]

    tap_order = [k for portion in PORTIONS for k in portion]
    weight = branch_kernel_weight.transpose(1, 0, 2)
    if branch == LANES and own_channels % 16 == 0:
        block = kernel_rows(weight, tap_order)
    else:
        block = jnp.concatenate([weight[k] for k in tap_order], axis=1)
    block, flat = together(block, features.reshape(pixels, channels))
    half_rows = channels // 2
    if paired:
        flat_own, flat_other = reordered(flat, me)
    else:
        to_relative = relative_order(channels, device_count, me)
        flat = dot_f32(flat, to_relative, 1, 0).astype(jnp.bfloat16)
        flat_own, flat_other = flat[:, :half_rows], flat[:, half_rows:]
    block = block.reshape(bits + block.shape)
    for bit in far_bits:
        (block,) = gathered([block], [bit], bit_count)
    flat_own, flat_other, merge_block = together(flat_own, flat_other, merge_weight)
    whole_merge = lax.all_to_all(
        jnp.broadcast_to(merge_block[None], (device_count,) + merge_block.shape), "row", 0, 0
    ).reshape(joined_width, merged_width)
    block, flat_own, flat_other = together(block, flat_own, flat_other)
    blocks = split(block, portion_widths)
    for step in range(len(orders[0])):
        if step == 1:
            *blocks, whole_merge = together(*blocks, whole_merge)
        else:
            blocks = together(*blocks)
        blocks = gathered(blocks, [o[step] for o in orders], bit_count)
    own_weight = [b.reshape(half_rows, b.shape[-1]) for b in blocks]

    def row_sum(parts):
        total = None
        for j, part in enumerate(parts):
            moved = column_shifted(part.reshape(rows, width, branch), (j - 1) * DILATION_RATE)
            total = moved if total is None else total + moved
        return total

    def by_tap(product):
        return split(product, [branch] * (product.shape[1] // branch))

    def product(own, other):
        return by_tap(dot_f32(flat_own, own, 1, 0) + dot_f32(flat_other, other, 1, 0))

    other_weight = [exchanged(w, 0) for w in own_weight[:2]]
    sums = [row_sum(product(a, b)) for a, b in zip(own_weight, other_weight)]
    own_weight[2], *sums = together(own_weight[2], *sums)
    other_weight.append(exchanged(own_weight[2], 0))
    centre = product(own_weight[2], other_weight[2])
    above = passed_along(sums[0], device_step)
    below = passed_along(sums[1], -device_step)
    z_dil = (row_sum(centre[1:]) + above + below).reshape(pixels, branch)
    act_one = jnp.maximum(centre[0] + branch_norm_bias[0], 0.0).astype(jnp.bfloat16)
    act_dil = jnp.maximum(z_dil + branch_norm_bias[1], 0.0).astype(jnp.bfloat16)
    joined = jnp.concatenate([act_one, act_dil], axis=1)
    merged = jnp.maximum(dot_f32(joined, whole_merge, 1, 0) + merge_bias, 0.0).astype(jnp.bfloat16)
    grad_out = jnp.where(
        merged > 0, cotangent.reshape(pixels, merged_width), jnp.zeros((), jnp.bfloat16)
    )
    back = dot_f32(grad_out, whole_merge, 1, 1)
    grad_one = jnp.where(act_one > 0, back[:, :branch], 0.0).astype(jnp.bfloat16)
    grad_dil = jnp.where(act_dil > 0, back[:, branch:], 0.0).astype(jnp.bfloat16)
    grad_map = grad_dil.reshape(rows, width, branch)
    halos = [passed_along(grad_map, -device_step), passed_along(grad_map, device_step)]

    def shifted_gradients(block):
        return [
            column_shifted(block, (1 - j) * DILATION_RATE).reshape(pixels, branch) for j in range(3)
        ]

    merge_total = dot_f32(joined, grad_out, 0, 0).astype(jnp.bfloat16)
    gradients = [None] * 3
    own_total, other_total = [None] * 3, [None] * 3
    for p in (2, 0, 1):
        parts = [grad_one] + shifted_gradients(grad_map) if p == 2 else shifted_gradients(halos[p])
        gradients[p] = jnp.concatenate(parts, axis=1)
        if p == 2:
            gradients[p], merge_total = together(gradients[p], merge_total)
            merge_parts = lax.all_to_all(
                merge_total.reshape(device_count, joined_rows, merged_width), "row", 0, 0
            )
        else:
            gradients[p] = lax.optimization_barrier(gradients[p])
        other_total[p] = dot_f32(flat_other, gradients[p], 0, 0).astype(jnp.bfloat16)
        own_total[p] = dot_f32(flat_own, gradients[p], 0, 0)
        if p == 2:
            *halos, own_total[2], other_total[2] = together(*halos, own_total[2], other_total[2])
    other_total = together(*other_total)
    arrived = together(*[exchanged(t, 0) for t in other_total])
    split_shape = (2,) * (bit_count - 1) + (own_channels, -1)
    totals = [
        added(t.reshape(split_shape), a.reshape(split_shape), o[-1], bit_count)
        for t, a, o in zip(own_total, arrived, orders)
    ]
    *sent, g0, g1, g2 = together(*[t[1] for t in totals], *gradients)
    if paired:
        input_grad = input_gradient([g0, g1, g2], own_weight, other_weight, me)
    else:
        input_total = sum(
            dot_f32(g, jnp.concatenate([a, b], axis=0), 1, 1)
            for g, a, b in zip((g0, g1, g2), own_weight, other_weight)
        ).astype(jnp.bfloat16)
        input_grad = dot_f32(input_total, to_relative, 1, 1).astype(jnp.bfloat16)
    for step in range(len(orders[0])):
        arrived = together(*[exchanged(t, o[-1 - step]) for t, o in zip(sent, orders)])
        if step == 0:
            *arrived, input_grad, merge_parts = together(*arrived, input_grad, merge_parts)
        own = [t[0] for t in totals]
        if step + 1 < len(orders[0]):
            totals = [
                added(t, a, o[-2 - step], bit_count) for t, a, o in zip(own, arrived, orders)
            ]
            sent = together(*[t[1] for t in totals])
        else:
            totals = [t + a.astype(jnp.float32) for t, a in zip(own, arrived)]
    grad_merge = jnp.sum(merge_parts.astype(jnp.float32), axis=0) * scale
    total = jnp.concatenate(totals, axis=-1)
    for bit in far_bits[::-1]:
        own, other = halves(total, bit, bit_count)
        total = own + exchanged(other, bit).astype(jnp.float32)
    weight_gradient = dict(
        zip([k for p in PORTIONS for k in p], by_tap(total.reshape(own_channels, -1)))
    )
    branch_kernel_gradient = jnp.stack([weight_gradient[k] for k in range(taps)], axis=1) * scale

    return (
        merged.reshape(rows, width, merged_width),
        input_grad.reshape(rows, width, channels),
        branch_kernel_gradient,
        grad_merge,
    )


def solution(mesh):
    placed = (
        P(("grp", "row"), None, None),
        P("row", None, None),
        P(),
        P("row", None),
        P(),
        P(("grp", "row"), None, None),
    )
    return jax.shard_map(
        on_device,
        mesh=mesh,
        in_specs=placed,
        out_specs=(
            P(("grp", "row"), None, None),
            P(("grp", "row"), None, None),
            P(("grp", "row"), None, None),
            P(("grp", "row"), None),
        ),
        check_vma=False,
    )
```

```python
import functools
import math

import jax
import jax.numpy as jnp
from jax import lax
from jax.experimental import pallas as pl
from jax.experimental.pallas import tpu as pltpu
from jax.sharding import PartitionSpec as P

DILATION_RATE = 18
LANES = 128
PORTIONS = ((1, 2, 3), (7, 8, 9), (0, 4, 5, 6))


def passed_along(block, distance):
    devices = range(lax.axis_size("row"))
    route = [(i - distance, i) for i in devices if i - distance in devices]
    return lax.ppermute(block, "row", route)


def exchanged(block, bit):
    return lax.ppermute(block, "row", [(i, i ^ (1 << bit)) for i in range(lax.axis_size("row"))])


def dot_f32(left, right, left_dim, right_dim):
    return lax.dot_general(
        left, right, (((left_dim,), (right_dim,)), ((), ())), preferred_element_type=jnp.float32
    )


def bit_orders(bit_count):
    near = [b for b in (3, 2, 1) if b < bit_count]
    return [near[k:] + near[:k] for k in range(3)]


def axis_of(bit, bit_count):
    return bit_count - 1 - bit


def after(value, *others):
    return lax.optimization_barrier((value,) + others)[0]


def together(*values):
    return list(lax.optimization_barrier(values))


def gathered(blocks, crossed, bit_count):
    arrived = together(*[exchanged(b, bit) for b, bit in zip(blocks, crossed)])
    return [
        jnp.concatenate([b, a], axis=axis_of(bit, bit_count))
        for b, a, bit in zip(blocks, arrived, crossed)
    ]


def added(own, arrived, bit, bit_count):
    axis = axis_of(bit, bit_count)

    def half(k):
        parts = [lax.slice_in_dim(x, k, k + 1, axis=axis) for x in (own, arrived)]
        return parts[0] + parts[1].astype(jnp.float32)

    return half(0), half(1).astype(jnp.bfloat16)


def halves(block, bit, bit_count):
    axis = axis_of(bit, bit_count)
    return (
        lax.slice_in_dim(block, 0, 1, axis=axis),
        lax.slice_in_dim(block, 1, 2, axis=axis).astype(jnp.bfloat16),
    )


def relative_order(size, device_count, me):
    width = size // device_count
    target = lax.broadcasted_iota(jnp.int32, (size, size), 1)
    source = lax.broadcasted_iota(jnp.int32, (size, size), 0)
    half = device_count // 2
    block, inner = target // width, target % width
    device = (block % half) * 2 + block // half
    return (source == (device ^ me) * width + inner).astype(jnp.bfloat16)


def reorder_kernel(me_ref, x_ref, own_ref, other_ref):
    me = me_ref[0]
    chip, core = me // 2, me % 2
    lane = lax.broadcasted_iota(jnp.int32, (x_ref.shape[0], LANES), 1)
    low_lane = lane < LANES // 2

    def tile(block):
        start = pl.multiple_of((block ^ chip) * LANES, LANES)
        return x_ref[:, pl.ds(start, LANES)].astype(jnp.float32)

    for t in range(own_ref.shape[1] // LANES):
        first, second = tile(2 * t), tile(2 * t + 1)
        low = jnp.where(low_lane, first, pltpu.roll(second, LANES // 2, 1)).astype(jnp.bfloat16)
        high = jnp.where(low_lane, pltpu.roll(first, LANES // 2, 1), second).astype(jnp.bfloat16)
        columns = slice(t * LANES, (t + 1) * LANES)
        own_ref[:, columns] = jnp.where(core == 0, low, high)
        other_ref[:, columns] = jnp.where(core == 0, high, low)


def reordered(flat, me):
    pixels, channels = flat.shape
    half = jax.ShapeDtypeStruct((pixels, channels // 2), flat.dtype)
    return pl.pallas_call(
        reorder_kernel,
        out_shape=(half, half),
        in_specs=[
            pl.BlockSpec(memory_space=pltpu.SMEM),
            pl.BlockSpec(memory_space=pltpu.VMEM),
        ],
        out_specs=(pl.BlockSpec(memory_space=pltpu.VMEM),) * 2,
        cost_estimate=pl.CostEstimate(
            flops=8 * pixels * channels, bytes_accessed=4 * pixels * channels, transcendentals=0
        ),
        compiler_params=pltpu.CompilerParams(vmem_limit_bytes=12 << 20),
        name="reorder",
    )(me.reshape(1), flat)


def kernel_rows_kernel(order, w_ref, out_ref):
    for place, k in enumerate(order):
        out_ref[:, place * LANES : (place + 1) * LANES] = w_ref[k]


def kernel_rows(weight, order):
    taps, rows, branch = weight.shape
    return pl.pallas_call(
        functools.partial(kernel_rows_kernel, order),
        out_shape=jax.ShapeDtypeStruct((rows, taps * branch), weight.dtype),
        in_specs=[pl.BlockSpec(memory_space=pltpu.VMEM)],
        out_specs=pl.BlockSpec(memory_space=pltpu.VMEM),
        cost_estimate=pl.CostEstimate(flops=0, bytes_accessed=4 * weight.size, transcendentals=0),
        compiler_params=pltpu.CompilerParams(vmem_limit_bytes=4 << 20),
        name="kernel_rows",
    )(weight)


def input_gradient_kernel(portion_count, me_ref, *refs):
    me = me_ref[0]
    chip, core = me // 2, me % 2
    gradients = refs[:portion_count]
    own, other = refs[portion_count : 2 * portion_count], refs[2 * portion_count : -1]
    out_ref = refs[-1]
    rows = LANES // 2

    def step(t, carry):
        total = None
        for p in range(portion_count):
            taken = []
            for k in range(2):
                at = pl.ds(pl.multiple_of(((2 * t + k) ^ chip) * rows, rows), rows)
                a, b = own[p][at, :], other[p][at, :]
                taken += [jnp.where(core == 0, a, b), jnp.where(core == 0, b, a)]
            part = dot_f32(gradients[p][...], jnp.concatenate(taken, axis=0), 1, 1)
            total = part if total is None else total + part
        columns = pl.ds(pl.multiple_of(t * 2 * LANES, 2 * LANES), 2 * LANES)
        out_ref[:, columns] = total.astype(out_ref.dtype)
        return carry

    lax.fori_loop(0, out_ref.shape[1] // (2 * LANES), step, 0, unroll=True)


def input_gradient(gradients, own, other, me):
    pixels = gradients[0].shape[0]
    half = own[0].shape[0]
    operands = [pltpu.with_memory_space_constraint(x, pltpu.VMEM) for x in (*gradients, *own, *other)]
    columns = sum(g.shape[1] for g in gradients)
    return pl.pallas_call(
        functools.partial(input_gradient_kernel, len(gradients)),
        out_shape=jax.ShapeDtypeStruct((pixels, 2 * half), jnp.bfloat16),
        in_specs=[pl.BlockSpec(memory_space=pltpu.SMEM)]
        + [pl.BlockSpec(memory_space=pltpu.VMEM)] * len(operands),
        out_specs=pl.BlockSpec(memory_space=pltpu.VMEM),
        cost_estimate=pl.CostEstimate(
            flops=4 * pixels * columns * half,
            bytes_accessed=2 * (pixels * columns + 2 * half * columns + 2 * pixels * half),
            transcendentals=0,
        ),
        compiler_params=pltpu.CompilerParams(vmem_limit_bytes=16 << 20),
        name="input_gradient",
    )(me.reshape(1), *operands)


def moved_rows(block, width, shift):
    if shift == 0:
        return block
    size = block.shape[0]
    column = lax.broadcasted_iota(jnp.int32, block.shape, 0) % width + shift
    inside = (column >= 0) & (column < width)
    return jnp.where(inside, pltpu.roll(block, (-shift) % size, 0), 0.0)


def head_kernel(
    width, centre_ref, above_ref, below_ref, bias_ref, merge_ref, merge_bias_ref, cotangent_ref,
    merged_ref, dilated_ref, gradient_ref, joined_ref, grad_out_ref,
):
    branch = above_ref.shape[1]
    z_dil = above_ref[...] + below_ref[...]
    for j in range(3):
        part = centre_ref[:, (1 + j) * branch : (2 + j) * branch]
        z_dil = z_dil + moved_rows(part, width, (j - 1) * DILATION_RATE)
    act_one = jnp.maximum(centre_ref[:, :branch] + bias_ref[0:1, :], 0.0).astype(jnp.bfloat16)
    act_dil = jnp.maximum(z_dil + bias_ref[1:2, :], 0.0).astype(jnp.bfloat16)
    joined = jnp.concatenate([act_one, act_dil], axis=1)
    joined_ref[...] = joined
    merged = jnp.maximum(dot_f32(joined, merge_ref[...], 1, 0) + merge_bias_ref[...], 0.0)
    merged = merged.astype(jnp.bfloat16)
    merged_ref[...] = merged
    cotangent = cotangent_ref[...].astype(jnp.float32)
    grad_out = jnp.where(merged.astype(jnp.float32) > 0, cotangent, 0.0).astype(jnp.bfloat16)
    grad_out_ref[...] = grad_out
    back = dot_f32(grad_out, merge_ref[...], 1, 1)
    kept = jnp.where(joined.astype(jnp.float32) > 0, back, 0.0).astype(jnp.bfloat16)
    dilated = kept[:, branch:]
    dilated_ref[...] = dilated
    gradient_ref[:, :branch] = kept[:, :branch]
    for j in range(3):
        moved = moved_rows(dilated.astype(jnp.float32), width, (1 - j) * DILATION_RATE)
        gradient_ref[:, (1 + j) * branch : (2 + j) * branch] = moved.astype(jnp.bfloat16)


def head(width, centre, above, below, bias, whole_merge, merge_bias, cotangent):
    pixels, branch = above.shape
    merged_width = whole_merge.shape[1]
    widths = (merged_width, branch, 4 * branch, 2 * branch, merged_width)
    operands = (centre, above, below, bias, whole_merge, merge_bias.reshape(1, -1), cotangent)
    return pl.pallas_call(
        functools.partial(head_kernel, width),
        out_shape=[jax.ShapeDtypeStruct((pixels, w), jnp.bfloat16) for w in widths],
        in_specs=[pl.BlockSpec(memory_space=pltpu.VMEM)] * len(operands),
        out_specs=[pl.BlockSpec(memory_space=pltpu.VMEM)] * len(widths),
        cost_estimate=pl.CostEstimate(
            flops=8 * pixels * branch * merged_width,
            bytes_accessed=8 * pixels * (6 * branch + merged_width),
            transcendentals=0,
        ),
        compiler_params=pltpu.CompilerParams(vmem_limit_bytes=12 << 20),
        name="head",
    )(*operands)


def shift_kernel(width, first_ref, second_ref, first_out_ref, second_out_ref):
    branch = first_ref.shape[1]
    for ref, out_ref in ((first_ref, first_out_ref), (second_ref, second_out_ref)):
        block = ref[...].astype(jnp.float32)
        for j in range(3):
            moved = moved_rows(block, width, (1 - j) * DILATION_RATE)
            out_ref[:, j * branch : (j + 1) * branch] = moved.astype(jnp.bfloat16)


def shifted(width, first, second):
    pixels, branch = first.shape
    out = jax.ShapeDtypeStruct((pixels, 3 * branch), jnp.bfloat16)
    return pl.pallas_call(
        functools.partial(shift_kernel, width),
        out_shape=(out, out),
        in_specs=[pl.BlockSpec(memory_space=pltpu.VMEM)] * 2,
        out_specs=(pl.BlockSpec(memory_space=pltpu.VMEM),) * 2,
        cost_estimate=pl.CostEstimate(
            flops=0, bytes_accessed=16 * pixels * branch, transcendentals=0
        ),
        compiler_params=pltpu.CompilerParams(vmem_limit_bytes=8 << 20),
        name="shift",
    )(first, second)


def merge_gradient_kernel(me_ref, joined_ref, grad_out_ref, own_ref, other_ref, total_ref):
    me = me_ref[0]
    total_ref[...] = dot_f32(joined_ref[...], grad_out_ref[...], 0, 0)
    half = own_ref.shape[0]
    group = 8
    for k in range(half // group):
        here = slice(k * group, (k + 1) * group)
        device = (2 * k) ^ me
        own_ref[here, :] = total_ref[pl.ds(pl.multiple_of(device * group, group), group), :]
        device = (2 * k + 1) ^ me
        other_ref[here, :] = total_ref[pl.ds(pl.multiple_of(device * group, group), group), :]


def merge_gradient(joined, grad_out, me):
    pixels, width = joined.shape
    half = jax.ShapeDtypeStruct((width // 2, grad_out.shape[1]), jnp.float32)
    return pl.pallas_call(
        merge_gradient_kernel,
        out_shape=(half, half),
        in_specs=[pl.BlockSpec(memory_space=pltpu.SMEM)]
        + [pl.BlockSpec(memory_space=pltpu.VMEM)] * 2,
        out_specs=(pl.BlockSpec(memory_space=pltpu.VMEM),) * 2,
        scratch_shapes=[pltpu.VMEM((width, grad_out.shape[1]), jnp.float32)],
        cost_estimate=pl.CostEstimate(
            flops=2 * pixels * width * grad_out.shape[1],
            bytes_accessed=8 * pixels * width,
            transcendentals=0,
        ),
        compiler_params=pltpu.CompilerParams(vmem_limit_bytes=8 << 20),
        name="merge_gradient",
    )(me.reshape(1), joined, grad_out)


def column_shifted(rows, shift):
    width = rows.shape[1]
    if shift == 0:
        return rows
    if shift > 0:
        return jnp.pad(rows[:, shift:], ((0, 0), (0, shift), (0, 0)))
    return jnp.pad(rows[:, : width + shift], ((0, 0), (-shift, 0), (0, 0)))


def on_device(
    features, branch_kernel_weight, branch_norm_bias, merge_weight, merge_bias, cotangent
):
    device_count = lax.axis_size("row")
    bit_count = device_count.bit_length() - 1
    me = lax.axis_index("row")
    rows, width, channels = features.shape
    taps, branch = branch_kernel_weight.shape[1:]
    own_channels = branch_kernel_weight.shape[0]
    joined_rows, merged_width = merge_weight.shape
    joined_width = joined_rows * device_count
    pixels = rows * width
    scale = 1.0 / math.sqrt(rows * device_count * width)
    device_step = DILATION_RATE // rows
    bits = (1,) * (bit_count - 1)
    orders = bit_orders(bit_count)
    far_bits = list(range(bit_count - 1, 3, -1))
    paired = 2 * own_channels == LANES and joined_rows == 8 and branch == LANES
    portion_widths = [len(p) * branch for p in PORTIONS]

    def split(array, widths):
        starts = [sum(widths[:i]) for i in range(len(widths))]
        return [lax.slice_in_dim(array, s, s + w, axis=-1) for s, w in zip(starts, widths)]

    tap_order = [k for portion in PORTIONS for k in portion]
    weight = branch_kernel_weight.transpose(1, 0, 2)
    if branch == LANES and own_channels % 16 == 0:
        block = kernel_rows(weight, tap_order)
    else:
        block = jnp.concatenate([weight[k] for k in tap_order], axis=1)
    block, flat, me = together(block, features.reshape(pixels, channels), me)
    half_rows = channels // 2
    if paired:
        flat_own, flat_other = reordered(flat, me)
    else:
        to_relative = relative_order(channels, device_count, me)
        flat = dot_f32(flat, to_relative, 1, 0).astype(jnp.bfloat16)
        flat_own, flat_other = flat[:, :half_rows], flat[:, half_rows:]
    block = block.reshape(bits + block.shape)
    merge_block = merge_weight.reshape(bits + merge_weight.shape)
    for bit in far_bits:
        block, merge_block = gathered([block, merge_block], [bit, bit], bit_count)
    block, flat_own, flat_other = together(block, flat_own, flat_other)
    blocks = split(block, portion_widths)
    blocks.append(merge_block)
    crossing = orders + [orders[0]]
    for step in range(len(orders[0])):
        blocks = gathered(together(*blocks), [o[step] for o in crossing], bit_count)
    own_merge = blocks.pop().reshape(joined_width // 2, merged_width)
    own_weight = [b.reshape(half_rows, b.shape[-1]) for b in blocks]

    def row_sum(parts):
        total = None
        for j, part in enumerate(parts):
            moved = column_shifted(part.reshape(rows, width, branch), (j - 1) * DILATION_RATE)
            total = moved if total is None else total + moved
        return total

    def by_tap(product):
        return split(product, [branch] * (product.shape[1] // branch))

    def product(own, other):
        return by_tap(dot_f32(flat_own, own, 1, 0) + dot_f32(flat_other, other, 1, 0))

    other_weight = [exchanged(w, 0) for w in own_weight[:2]]
    sums = [row_sum(product(a, b)) for a, b in zip(own_weight, other_weight)]
    merge_to_relative = relative_order(joined_width, device_count, me)
    own_weight[2], own_merge, *sums = together(own_weight[2], own_merge, *sums)
    whole_merge = dot_f32(
        merge_to_relative, jnp.concatenate([own_merge, exchanged(own_merge, 0)], axis=0), 1, 0
    ).astype(jnp.bfloat16)
    other_weight.append(exchanged(own_weight[2], 0))
    centre = dot_f32(flat_own, own_weight[2], 1, 0) + dot_f32(flat_other, other_weight[2], 1, 0)
    above = passed_along(sums[0], device_step).reshape(pixels, branch)
    below = passed_along(sums[1], -device_step).reshape(pixels, branch)
    flat_cotangent = cotangent.reshape(pixels, merged_width)
    if paired:
        merged, grad_dil, centre_gradient, joined, grad_out = head(
            width, centre, above, below, branch_norm_bias, whole_merge, merge_bias, flat_cotangent
        )
    else:
        centre = by_tap(centre)
        z_dil = row_sum(centre[1:]).reshape(pixels, branch) + above + below
        act_one = jnp.maximum(centre[0] + branch_norm_bias[0], 0.0).astype(jnp.bfloat16)
        act_dil = jnp.maximum(z_dil + branch_norm_bias[1], 0.0).astype(jnp.bfloat16)
        joined = jnp.concatenate([act_one, act_dil], axis=1)
        merged = jnp.maximum(dot_f32(joined, whole_merge, 1, 0) + merge_bias, 0.0)
        merged = merged.astype(jnp.bfloat16)
        grad_out = jnp.where(merged > 0, flat_cotangent, jnp.zeros((), jnp.bfloat16))
        back = dot_f32(grad_out, whole_merge, 1, 1)
        kept = jnp.where(joined > 0, back, 0.0).astype(jnp.bfloat16)
        grad_dil = kept[:, branch:]
        centre_gradient = None

    def shifted_gradients(block):
        block = block.reshape(rows, width, branch)
        parts = [column_shifted(block, (1 - j) * DILATION_RATE) for j in range(3)]
        return [part.reshape(pixels, branch) for part in parts]

    if not paired:
        centre_gradient = jnp.concatenate([kept[:, :branch]] + shifted_gradients(grad_dil), axis=1)
    halos = [passed_along(grad_dil, -device_step), passed_along(grad_dil, device_step)]
    if paired:
        own_merge, other_merge = merge_gradient(joined, grad_out, me)
    else:
        joined_relative = dot_f32(joined, merge_to_relative, 1, 0).astype(jnp.bfloat16)
        merge_total = dot_f32(joined_relative, grad_out, 0, 0)
        own_merge = merge_total[: joined_width // 2]
        other_merge = merge_total[joined_width // 2 :]
    merge_arrived = exchanged(other_merge, 0)

    centre_gradient, own_merge = together(centre_gradient, own_merge)
    own_total, other_total = [None] * 3, [None] * 3
    other_total[2] = dot_f32(flat_other, centre_gradient, 0, 0).astype(jnp.bfloat16)
    own_total[2] = dot_f32(flat_own, centre_gradient, 0, 0)
    *halos, own_total[2], other_total[2] = together(*halos, own_total[2], other_total[2])
    if paired:
        gradients = [*shifted(width, *halos), centre_gradient]
    else:
        gradients = [jnp.concatenate(shifted_gradients(h), axis=1) for h in halos]
        gradients = together(*gradients) + [centre_gradient]
    for p in range(2):
        other_total[p] = dot_f32(flat_other, gradients[p], 0, 0).astype(jnp.bfloat16)
        own_total[p] = dot_f32(flat_own, gradients[p], 0, 0)
    merge_total = own_merge + merge_arrived.astype(jnp.float32)
    merge_total = merge_total.reshape((2,) * (bit_count - 1) + (joined_rows, merged_width))
    merge_parts = halves(merge_total, far_bits[0], bit_count) if far_bits else None
    sending = list(other_total) + ([merge_parts[1]] if far_bits else [])
    arrived = [
        exchanged(t, b) for t, b in zip(together(*sending), [0, 0, 0] + far_bits[:1])
    ]
    arrived = together(*arrived)
    if far_bits:
        merge_total = merge_parts[0] + arrived.pop().astype(jnp.float32)
    for bit in far_bits[1:]:
        own, other = halves(merge_total, bit, bit_count)
        merge_total = own + exchanged(other, bit).astype(jnp.float32)
    totals = []
    for own, a, o in zip(own_total, arrived, orders):
        shape = (2,) * (bit_count - 1) + (own.shape[0] // (device_count // 2), own.shape[1])
        totals.append(added(own.reshape(shape), a.reshape(shape), o[-1], bit_count))
    totals.append(halves(merge_total, crossing[3][-1], bit_count))
    *sent, g0, g1, g2 = together(*[t[1] for t in totals], *gradients)
    if paired:
        input_grad = input_gradient([g0, g1, g2], own_weight, other_weight, me)
    else:
        input_total = sum(
            dot_f32(g, jnp.concatenate([a, b], axis=0), 1, 1)
            for g, a, b in zip((g0, g1, g2), own_weight, other_weight)
        ).astype(jnp.bfloat16)
        input_grad = dot_f32(input_total, to_relative, 1, 1).astype(jnp.bfloat16)
    for step in range(len(orders[0])):
        arrived = together(*[exchanged(t, o[-1 - step]) for t, o in zip(sent, crossing)])
        if step == 0:
            *arrived, input_grad = together(*arrived, input_grad)
        own = [t[0] for t in totals]
        if step + 1 < len(orders[0]):
            totals = [
                added(t, a, o[-2 - step], bit_count) for t, a, o in zip(own, arrived, crossing)
            ]
            sent = together(*[t[1] for t in totals])
        else:
            totals = [t + a.astype(jnp.float32) for t, a in zip(own, arrived)]
    grad_merge = totals[3].reshape(joined_rows, merged_width) * scale
    total = jnp.concatenate(totals[:3], axis=-1)
    for bit in far_bits[::-1]:
        own, other = halves(total, bit, bit_count)
        total = own + exchanged(other, bit).astype(jnp.float32)
    weight_gradient = dict(
        zip([k for p in PORTIONS for k in p], by_tap(total.reshape(own_channels, -1)))
    )
    branch_kernel_gradient = jnp.stack([weight_gradient[k] for k in range(taps)], axis=1) * scale

    return (
        merged.reshape(rows, width, merged_width),
        input_grad.reshape(rows, width, channels),
        branch_kernel_gradient,
        grad_merge,
    )


def solution(mesh):
    placed = (
        P(("grp", "row"), None, None),
        P("row", None, None),
        P(),
        P("row", None),
        P(),
        P(("grp", "row"), None, None),
    )
    return jax.shard_map(
        on_device,
        mesh=mesh,
        in_specs=placed,
        out_specs=(
            P(("grp", "row"), None, None),
            P(("grp", "row"), None, None),
            P(("grp", "row"), None, None),
            P(("grp", "row"), None),
        ),
        check_vma=False,
    )
```

```python
import functools
import math

import jax
import jax.numpy as jnp
from jax import lax
from jax.experimental import pallas as pl
from jax.experimental.pallas import tpu as pltpu
from jax.sharding import PartitionSpec as P

DILATION_RATE = 18
LANES = 128
PORTIONS = ((1, 2, 3), (7, 8, 9), (0, 4, 5, 6))


def swapped(block, distance, parity):
    count = lax.axis_size("row")
    pairs = [(i, i + distance) for i in range(count - distance) if i // distance % 2 == parity]
    return lax.ppermute(block, "row", pairs + [(b, a) for a, b in pairs])


def exchanged(block, bit):
    return lax.ppermute(block, "row", [(i, i ^ (1 << bit)) for i in range(lax.axis_size("row"))])


def dot_f32(left, right, left_dim, right_dim):
    return lax.dot_general(
        left, right, (((left_dim,), (right_dim,)), ((), ())), preferred_element_type=jnp.float32
    )


def bit_orders(bit_count):
    near = [b for b in (3, 2, 1) if b < bit_count]
    return [near[k:] + near[:k] for k in range(3)]


def axis_of(bit, bit_count):
    return bit_count - 1 - bit


def after(value, *others):
    return lax.optimization_barrier((value,) + others)[0]


def together(*values):
    return list(lax.optimization_barrier(values))


def gathered(blocks, crossed, bit_count):
    arrived = together(*[exchanged(b, bit) for b, bit in zip(blocks, crossed)])
    return [
        jnp.concatenate([b, a], axis=axis_of(bit, bit_count))
        for b, a, bit in zip(blocks, arrived, crossed)
    ]


def added(own, arrived, bit, bit_count):
    axis = axis_of(bit, bit_count)

    def half(k):
        parts = [lax.slice_in_dim(x, k, k + 1, axis=axis) for x in (own, arrived)]
        return parts[0] + parts[1].astype(jnp.float32)

    return half(0), half(1).astype(jnp.bfloat16)


def halves(block, bit, bit_count):
    axis = axis_of(bit, bit_count)
    return (
        lax.slice_in_dim(block, 0, 1, axis=axis),
        lax.slice_in_dim(block, 1, 2, axis=axis).astype(jnp.bfloat16),
    )


def relative_order(size, device_count, me):
    width = size // device_count
    target = lax.broadcasted_iota(jnp.int32, (size, size), 1)
    source = lax.broadcasted_iota(jnp.int32, (size, size), 0)
    half = device_count // 2
    block, inner = target // width, target % width
    device = (block % half) * 2 + block // half
    return (source == (device ^ me) * width + inner).astype(jnp.bfloat16)


def reorder_kernel(me_ref, x_ref, own_ref, other_ref):
    me = me_ref[0]
    chip, core = me // 2, me % 2
    lane = lax.broadcasted_iota(jnp.int32, (x_ref.shape[0], LANES), 1)
    low_lane = lane < LANES // 2

    def tile(block):
        start = pl.multiple_of((block ^ chip) * LANES, LANES)
        return x_ref[:, pl.ds(start, LANES)].astype(jnp.float32)

    for t in range(own_ref.shape[1] // LANES):
        first, second = tile(2 * t), tile(2 * t + 1)
        low = jnp.where(low_lane, first, pltpu.roll(second, LANES // 2, 1)).astype(jnp.bfloat16)
        high = jnp.where(low_lane, pltpu.roll(first, LANES // 2, 1), second).astype(jnp.bfloat16)
        columns = slice(t * LANES, (t + 1) * LANES)
        own_ref[:, columns] = jnp.where(core == 0, low, high)
        other_ref[:, columns] = jnp.where(core == 0, high, low)


def reordered(flat, me):
    pixels, channels = flat.shape
    half = jax.ShapeDtypeStruct((pixels, channels // 2), flat.dtype)
    return pl.pallas_call(
        reorder_kernel,
        out_shape=(half, half),
        in_specs=[
            pl.BlockSpec(memory_space=pltpu.SMEM),
            pl.BlockSpec(memory_space=pltpu.VMEM),
        ],
        out_specs=(pl.BlockSpec(memory_space=pltpu.VMEM),) * 2,
        cost_estimate=pl.CostEstimate(
            flops=8 * pixels * channels, bytes_accessed=4 * pixels * channels, transcendentals=0
        ),
        compiler_params=pltpu.CompilerParams(vmem_limit_bytes=12 << 20),
        name="reorder",
    )(me.reshape(1), flat)


def input_gradient_kernel(portion_count, me_ref, *refs):
    me = me_ref[0]
    chip, core = me // 2, me % 2
    gradients = refs[:portion_count]
    own, other = refs[portion_count : 2 * portion_count], refs[2 * portion_count : -1]
    out_ref = refs[-1]
    rows = LANES // 2

    def step(t, carry):
        total = None
        for p in range(portion_count):
            taken = []
            for k in range(2):
                at = pl.ds(pl.multiple_of(((2 * t + k) ^ chip) * rows, rows), rows)
                a, b = own[p][at, :], other[p][at, :]
                taken += [jnp.where(core == 0, a, b), jnp.where(core == 0, b, a)]
            part = dot_f32(gradients[p][...], jnp.concatenate(taken, axis=0), 1, 1)
            total = part if total is None else total + part
        columns = pl.ds(pl.multiple_of(t * 2 * LANES, 2 * LANES), 2 * LANES)
        out_ref[:, columns] = total.astype(out_ref.dtype)
        return carry

    lax.fori_loop(0, out_ref.shape[1] // (2 * LANES), step, 0, unroll=True)


def input_gradient(gradients, own, other, me):
    pixels = gradients[0].shape[0]
    half = own[0].shape[0]
    operands = [pltpu.with_memory_space_constraint(x, pltpu.VMEM) for x in (*gradients, *own, *other)]
    columns = sum(g.shape[1] for g in gradients)
    return pl.pallas_call(
        functools.partial(input_gradient_kernel, len(gradients)),
        out_shape=jax.ShapeDtypeStruct((pixels, 2 * half), jnp.bfloat16),
        in_specs=[pl.BlockSpec(memory_space=pltpu.SMEM)]
        + [pl.BlockSpec(memory_space=pltpu.VMEM)] * len(operands),
        out_specs=pl.BlockSpec(memory_space=pltpu.VMEM),
        cost_estimate=pl.CostEstimate(
            flops=4 * pixels * columns * half,
            bytes_accessed=2 * (pixels * columns + 2 * half * columns + 2 * pixels * half),
            transcendentals=0,
        ),
        compiler_params=pltpu.CompilerParams(vmem_limit_bytes=16 << 20),
        name="input_gradient",
    )(me.reshape(1), *operands)


def moved_rows(block, width, shift):
    if shift == 0:
        return block
    size = block.shape[0]
    column = lax.broadcasted_iota(jnp.int32, block.shape, 0) % width + shift
    inside = (column >= 0) & (column < width)
    return jnp.where(inside, pltpu.roll(block, (-shift) % size, 0), 0.0)


def head_kernel(
    width, centre_ref, above_ref, below_ref, bias_ref, merge_ref, merge_bias_ref, cotangent_ref,
    merged_ref, dilated_ref, gradient_ref, joined_ref, grad_out_ref,
):
    branch = above_ref.shape[1]
    z_dil = above_ref[...] + below_ref[...]
    for j in range(3):
        part = centre_ref[:, (1 + j) * branch : (2 + j) * branch]
        z_dil = z_dil + moved_rows(part, width, (j - 1) * DILATION_RATE)
    act_one = jnp.maximum(centre_ref[:, :branch] + bias_ref[0:1, :], 0.0).astype(jnp.bfloat16)
    act_dil = jnp.maximum(z_dil + bias_ref[1:2, :], 0.0).astype(jnp.bfloat16)
    joined = jnp.concatenate([act_one, act_dil], axis=1)
    joined_ref[...] = joined
    merged = jnp.maximum(dot_f32(joined, merge_ref[...], 1, 0) + merge_bias_ref[...], 0.0)
    merged = merged.astype(jnp.bfloat16)
    merged_ref[...] = merged
    cotangent = cotangent_ref[...].astype(jnp.float32)
    grad_out = jnp.where(merged.astype(jnp.float32) > 0, cotangent, 0.0).astype(jnp.bfloat16)
    grad_out_ref[...] = grad_out
    back = dot_f32(grad_out, merge_ref[...], 1, 1)
    kept = jnp.where(joined.astype(jnp.float32) > 0, back, 0.0).astype(jnp.bfloat16)
    dilated = kept[:, branch:]
    dilated_ref[...] = dilated
    gradient_ref[:, :branch] = kept[:, :branch]
    for j in range(3):
        moved = moved_rows(dilated.astype(jnp.float32), width, (1 - j) * DILATION_RATE)
        gradient_ref[:, (1 + j) * branch : (2 + j) * branch] = moved.astype(jnp.bfloat16)


def head(width, centre, above, below, bias, whole_merge, merge_bias, cotangent):
    pixels, branch = above.shape
    merged_width = whole_merge.shape[1]
    widths = (merged_width, branch, 4 * branch, 2 * branch, merged_width)
    operands = (centre, above, below, bias, whole_merge, merge_bias.reshape(1, -1), cotangent)
    return pl.pallas_call(
        functools.partial(head_kernel, width),
        out_shape=[jax.ShapeDtypeStruct((pixels, w), jnp.bfloat16) for w in widths],
        in_specs=[pl.BlockSpec(memory_space=pltpu.VMEM)] * len(operands),
        out_specs=[pl.BlockSpec(memory_space=pltpu.VMEM)] * len(widths),
        cost_estimate=pl.CostEstimate(
            flops=8 * pixels * branch * merged_width,
            bytes_accessed=8 * pixels * (6 * branch + merged_width),
            transcendentals=0,
        ),
        compiler_params=pltpu.CompilerParams(vmem_limit_bytes=12 << 20),
        name="head",
    )(*operands)


def is_upward(me, step):
    return me // step % 2 == 0


def halo_kernel(width, step, me_ref, first_ref, second_ref, first_out_ref, second_out_ref):
    branch = first_out_ref.shape[1]
    sums = []
    for ref in (first_ref, second_ref):
        total = None
        for j in range(3):
            part = ref[:, j * branch : (j + 1) * branch]
            moved = moved_rows(part, width, (j - 1) * DILATION_RATE)
            total = moved if total is None else total + moved
        sums.append(total)
    upward = is_upward(me_ref[0], step)
    first_out_ref[...] = jnp.where(upward, sums[0], sums[1])
    second_out_ref[...] = jnp.where(upward, sums[1], sums[0])


def halo_sums(width, step, products, me):
    pixels, taps = products[0].shape
    out = jax.ShapeDtypeStruct((pixels, taps // 3), jnp.float32)
    return halo_call(functools.partial(halo_kernel, width, step), "halo_sums", out, me, *products)


def shift_kernel(width, step, me_ref, first_ref, second_ref, first_out_ref, second_out_ref):
    branch = first_ref.shape[1]
    upward = is_upward(me_ref[0], step)
    first, second = first_ref[...].astype(jnp.float32), second_ref[...].astype(jnp.float32)
    pairs = ((first, second, first_out_ref), (second, first, second_out_ref))
    for here, there, out_ref in pairs:
        block = jnp.where(upward, here, there)
        for j in range(3):
            moved = moved_rows(block, width, (1 - j) * DILATION_RATE)
            out_ref[:, j * branch : (j + 1) * branch] = moved.astype(jnp.bfloat16)


def shifted(width, step, first, second, me):
    pixels, branch = first.shape
    out = jax.ShapeDtypeStruct((pixels, 3 * branch), jnp.bfloat16)
    return halo_call(functools.partial(shift_kernel, width, step), "shift", out, me, first, second)


def halo_call(kernel, name, out, me, first, second):
    return pl.pallas_call(
        kernel,
        out_shape=(out, out),
        in_specs=[pl.BlockSpec(memory_space=pltpu.SMEM)]
        + [pl.BlockSpec(memory_space=pltpu.VMEM)] * 2,
        out_specs=(pl.BlockSpec(memory_space=pltpu.VMEM),) * 2,
        cost_estimate=pl.CostEstimate(
            flops=0, bytes_accessed=8 * (first.size + out.size), transcendentals=0
        ),
        compiler_params=pltpu.CompilerParams(vmem_limit_bytes=8 << 20),
        name=name,
    )(me.reshape(1), first, second)


def merge_gradient_kernel(me_ref, joined_ref, grad_out_ref, own_ref, other_ref, total_ref):
    me = me_ref[0]
    total_ref[...] = dot_f32(joined_ref[...], grad_out_ref[...], 0, 0)
    half = own_ref.shape[0]
    group = 8
    for k in range(half // group):
        here = slice(k * group, (k + 1) * group)
        device = (2 * k) ^ me
        own_ref[here, :] = total_ref[pl.ds(pl.multiple_of(device * group, group), group), :]
        device = (2 * k + 1) ^ me
        other_ref[here, :] = total_ref[pl.ds(pl.multiple_of(device * group, group), group), :]


def merge_gradient(joined, grad_out, me):
    pixels, width = joined.shape
    half = jax.ShapeDtypeStruct((width // 2, grad_out.shape[1]), jnp.float32)
    return pl.pallas_call(
        merge_gradient_kernel,
        out_shape=(half, half),
        in_specs=[pl.BlockSpec(memory_space=pltpu.SMEM)]
        + [pl.BlockSpec(memory_space=pltpu.VMEM)] * 2,
        out_specs=(pl.BlockSpec(memory_space=pltpu.VMEM),) * 2,
        scratch_shapes=[pltpu.VMEM((width, grad_out.shape[1]), jnp.float32)],
        cost_estimate=pl.CostEstimate(
            flops=2 * pixels * width * grad_out.shape[1],
            bytes_accessed=8 * pixels * width,
            transcendentals=0,
        ),
        compiler_params=pltpu.CompilerParams(vmem_limit_bytes=8 << 20),
        name="merge_gradient",
    )(me.reshape(1), joined, grad_out)


def layout(rows, merge_rows, merge_width):
    shares = (0, 3 * rows // 8, 6 * rows // 8, rows)
    tables = []
    for p, portion in enumerate(PORTIONS):
        table = [(k, 0, n * rows, rows) for n, k in enumerate(k for k in portion if k > 0)]
        table.append((0, shares[p], 3 * rows, shares[p + 1] - shares[p]))
        if p == 2:
            first = 3 * rows + table[-1][3]
            lanes = range(0, merge_width, LANES)
            table += [(None, x, first + n * merge_rows, merge_rows) for n, x in enumerate(lanes)]
        tables.append(table)
    return tables


def stack_rows(table):
    return table[-1][2] + table[-1][3]


def lanes_of(k):
    for p, portion in enumerate(PORTIONS):
        if k in portion:
            at = portion.index(k) * LANES
            return p, slice(at, at + LANES)


def local_call(kernel, name, out_shape, operands, moved, grant):
    return pl.pallas_call(
        kernel,
        out_shape=out_shape,
        in_specs=[pl.BlockSpec(memory_space=pltpu.VMEM)] * len(operands),
        out_specs=[pl.BlockSpec(memory_space=pltpu.VMEM)] * len(out_shape),
        cost_estimate=pl.CostEstimate(flops=moved // 4, bytes_accessed=moved, transcendentals=0),
        compiler_params=pltpu.CompilerParams(vmem_limit_bytes=grant << 20),
        name=name,
    )(*operands)


def pack_kernel(tables, weight_ref, merge_ref, out_ref):
    base = 0
    for table in tables:
        for k, there, here, count in table:
            at = slice(base + here, base + here + count)
            if k is None:
                out_ref[at, :] = merge_ref[:, there : there + LANES]
            else:
                out_ref[at, :] = weight_ref[k, there : there + count, :]
        base += stack_rows(table)


def pack(weight, merge_weight, tables):
    out = [jax.ShapeDtypeStruct((sum(map(stack_rows, tables)), LANES), weight.dtype)]
    kernel = functools.partial(pack_kernel, tables)
    return local_call(kernel, "pack", out, (weight, merge_weight), 4 * weight.size, 4)[0]


def block_pair(target, inner):
    low = target // inner * (2 * inner) + target % inner
    return low, low + inner


def unpack_kernel(tables, inners, *refs):
    outs = refs[6:]

    def step(target, carry):
        for p, table in enumerate(tables):
            for ref, block in zip(refs[2 * p : 2 * p + 2], block_pair(target, inners[p])):
                for k, there, here, count in table:
                    value = ref[target, here : here + count, :]
                    if k is None:
                        outs[3][block, :, there : there + LANES] = value
                    else:
                        q, lanes = lanes_of(k)
                        outs[q][block, there : there + count, lanes] = value
        return carry

    lax.fori_loop(0, refs[0].shape[0], step, 0)


def unpack(pairs, tables, inners, rows, merge_rows, merge_width):
    blocks = 2 * pairs[0].shape[0]
    shapes = [(blocks, rows, LANES * len(p)) for p in PORTIONS] + [(blocks, merge_rows, merge_width)]
    out = [jax.ShapeDtypeStruct(x, jnp.bfloat16) for x in shapes]
    kernel = functools.partial(unpack_kernel, tables, tuple(inners))
    return local_call(kernel, "unpack", out, pairs, 4 * sum(x.size for x in pairs), 16)


def first_fold_kernel(tables, inners, *refs):
    owns, arriveds, keeps, sends = refs[:4], refs[4:8], refs[8:11], refs[11:]

    def step(target, carry):
        for p, table in enumerate(tables):
            for half, block in enumerate(block_pair(target, inners[p])):
                for k, there, here, count in table:
                    if k is None:
                        q, at = 3, (block, slice(None), slice(there, there + LANES))
                    else:
                        q, lanes = lanes_of(k)
                        at = (block, slice(there, there + count), lanes)
                    value = owns[q][at] + arriveds[q][at].astype(jnp.float32)
                    out_ref = (keeps, sends)[half][p]
                    out_ref[target, here : here + count, :] = value.astype(out_ref.dtype)
        return carry

    lax.fori_loop(0, keeps[0].shape[0], step, 0)


def fold_kernel(inners, *refs):
    owns, arriveds, keeps, sends = (refs[3 * k : 3 * k + 3] for k in range(4))

    def step(target, carry):
        for p in range(3):
            for half, block in enumerate(block_pair(target, inners[p])):
                value = owns[p][block] + arriveds[p][block].astype(jnp.float32)
                out_ref = (keeps, sends)[half][p]
                out_ref[target] = value.astype(out_ref.dtype)
        return carry

    lax.fori_loop(0, keeps[0].shape[0], step, 0)


def fold(owns, arriveds, tables, inners):
    shapes = [(owns[0].shape[0] // 2, stack_rows(table), LANES) for table in tables]
    out = [jax.ShapeDtypeStruct(x, t) for t in (jnp.float32, jnp.bfloat16) for x in shapes]
    if len(owns) == 4:
        kernel = functools.partial(first_fold_kernel, tables, tuple(inners))
    else:
        kernel = functools.partial(fold_kernel, tuple(inners))
    moved = 9 * sum(x.size for x in owns)
    out = local_call(kernel, "fold", out, (*owns, *arriveds), moved, 20)
    return out[:3], out[3:]


def last_fold_kernel(*refs):
    owns, arriveds = refs[:3], refs[3:6]
    base = 0
    for own, arrived in zip(owns, arriveds):
        at = slice(base, base + own.shape[1])
        base += own.shape[1]
        refs[6][at, :] = own[0] + arrived[0].astype(jnp.float32)
        refs[7][at, :] = (own[1] + arrived[1].astype(jnp.float32)).astype(jnp.bfloat16)


def last_fold(owns, arriveds):
    shape = (sum(x.shape[1] for x in owns), LANES)
    out = [jax.ShapeDtypeStruct(shape, t) for t in (jnp.float32, jnp.bfloat16)]
    moved = 9 * sum(x.size for x in owns)
    return local_call(last_fold_kernel, "last_fold", out, (*owns, *arriveds), moved, 8)


def scaled_kernel(tables, scale, keep_ref, arrived_ref, out_ref, out_merge_ref):
    base = 0
    for table in tables:
        for k, there, here, count in table:
            at = slice(base + here, base + here + count)
            value = (keep_ref[at, :] + arrived_ref[at, :].astype(jnp.float32)) * scale
            if k is None:
                out_merge_ref[:, there : there + LANES] = value
            else:
                out_ref[k, there : there + count, :] = value
        base += stack_rows(table)


def scaled(keep, arrived, tables, scale, rows, merge_rows, merge_width):
    taps = sum(map(len, PORTIONS))
    out = [
        jax.ShapeDtypeStruct((taps, rows, LANES), jnp.float32),
        jax.ShapeDtypeStruct((merge_rows, merge_width), jnp.float32),
    ]
    kernel = functools.partial(scaled_kernel, tables, scale)
    return local_call(kernel, "scaled", out, (keep, arrived), 10 * keep.size, 8)


def column_shifted(rows, shift):
    width = rows.shape[1]
    if shift == 0:
        return rows
    if shift > 0:
        return jnp.pad(rows[:, shift:], ((0, 0), (0, shift), (0, 0)))
    return jnp.pad(rows[:, : width + shift], ((0, 0), (-shift, 0), (0, 0)))


def on_device(
    features, branch_kernel_weight, branch_norm_bias, merge_weight, merge_bias, cotangent
):
    device_count = lax.axis_size("row")
    bit_count = device_count.bit_length() - 1
    me = lax.axis_index("row")
    rows, width, channels = features.shape
    taps, branch = branch_kernel_weight.shape[1:]
    own_channels = branch_kernel_weight.shape[0]
    joined_rows, merged_width = merge_weight.shape
    joined_width = joined_rows * device_count
    pixels = rows * width
    scale = 1.0 / math.sqrt(rows * device_count * width)
    device_step = DILATION_RATE // rows
    bits = (1,) * (bit_count - 1)
    orders = bit_orders(bit_count)
    far_bits = list(range(bit_count - 1, 3, -1))
    paired = 2 * own_channels == LANES and joined_rows == 8 and branch == LANES and bit_count == 5
    portion_widths = [len(p) * branch for p in PORTIONS]

    def split(array, widths):
        starts = [sum(widths[:i]) for i in range(len(widths))]
        return [lax.slice_in_dim(array, s, s + w, axis=-1) for s, w in zip(starts, widths)]

    tap_order = [k for portion in PORTIONS for k in portion]
    weight = branch_kernel_weight.transpose(1, 0, 2)
    half_rows = channels // 2
    crossing = orders + [orders[1]]
    flat = features.reshape(pixels, channels)
    if paired:
        tables = layout(own_channels, joined_rows, merged_width)
        block = pack(weight, merge_weight, tables)
        block, flat, me = together(block, flat, me)
        flat_own, flat_other = reordered(flat, me)
        block = block.reshape(bits + block.shape)
        (arrived,) = together(exchanged(block, far_bits[0]))
        block, arrived, flat_own, flat_other = together(block, arrived, flat_own, flat_other)
        blocks, base = [], 0
        for table in tables:
            parts = [
                lax.slice_in_dim(x, base, base + stack_rows(table), axis=-2) for x in (block, arrived)
            ]
            blocks.append(jnp.concatenate(parts, axis=0))
            base += stack_rows(table)
        for step in range(len(orders[0]) - 1):
            blocks = gathered(together(*blocks), [o[step] for o in orders], bit_count)
        blocks = together(*blocks)
        arrived = together(*[exchanged(b, o[-1]) for b, o in zip(blocks, orders)])
        pairs = [
            x.reshape((device_count // 4,) + x.shape[-2:])
            for pair in zip(blocks, arrived)
            for x in pair
        ]
        inners = [1 << (o[-1] - 1) for o in orders]
        *own_weight, own_merge = unpack(
            pairs, tables, inners, own_channels, joined_rows, merged_width
        )
        own_weight = [x.reshape(half_rows, x.shape[-1]) for x in own_weight]
    else:
        block = jnp.concatenate([weight[k] for k in tap_order], axis=1)
        to_relative = relative_order(channels, device_count, me)
        flat = dot_f32(flat, to_relative, 1, 0).astype(jnp.bfloat16)
        flat_own, flat_other = flat[:, :half_rows], flat[:, half_rows:]
        block = block.reshape(bits + block.shape)
        merge_block = merge_weight.reshape(bits + merge_weight.shape)
        for bit in far_bits:
            block, merge_block = gathered([block, merge_block], [bit, bit], bit_count)
        blocks = split(block, portion_widths) + [merge_block]
        for step in range(len(orders[0])):
            blocks = gathered(together(*blocks), [o[step] for o in crossing], bit_count)
        own_merge = blocks.pop()
        own_weight = [b.reshape(half_rows, b.shape[-1]) for b in blocks]
    own_merge = own_merge.reshape(joined_width // 2, merged_width)

    def row_sum(parts):
        total = None
        for j, part in enumerate(parts):
            moved = column_shifted(part.reshape(rows, width, branch), (j - 1) * DILATION_RATE)
            total = moved if total is None else total + moved
        return total

    def by_tap(product):
        return split(product, [branch] * (product.shape[1] // branch))

    other_weight = [exchanged(w, 0) for w in own_weight[:2]]
    sums = [
        dot_f32(flat_own, a, 1, 0) + dot_f32(flat_other, b, 1, 0)
        for a, b in zip(own_weight, other_weight)
    ]
    upward = is_upward(me, device_step)
    if paired:
        sums = halo_sums(width, device_step, sums, me)
    else:
        sums = [row_sum(by_tap(x)).reshape(pixels, branch) for x in sums]
        sums = [jnp.where(upward, *sums), jnp.where(upward, *sums[::-1])]
    merge_to_relative = relative_order(joined_width, device_count, me)
    own_weight[2], own_merge, *sums = together(own_weight[2], own_merge, *sums)
    whole_merge = dot_f32(
        merge_to_relative, jnp.concatenate([own_merge, exchanged(own_merge, 0)], axis=0), 1, 0
    ).astype(jnp.bfloat16)
    other_weight.append(exchanged(own_weight[2], 0))
    centre = dot_f32(flat_own, own_weight[2], 1, 0) + dot_f32(flat_other, other_weight[2], 1, 0)
    above, below = swapped(sums[0], device_step, 0), swapped(sums[1], device_step, 1)
    flat_cotangent = cotangent.reshape(pixels, merged_width)
    if paired:
        merged, grad_dil, centre_gradient, joined, grad_out = head(
            width, centre, above, below, branch_norm_bias, whole_merge, merge_bias, flat_cotangent
        )
    else:
        centre = by_tap(centre)
        z_dil = row_sum(centre[1:]).reshape(pixels, branch) + above + below
        act_one = jnp.maximum(centre[0] + branch_norm_bias[0], 0.0).astype(jnp.bfloat16)
        act_dil = jnp.maximum(z_dil + branch_norm_bias[1], 0.0).astype(jnp.bfloat16)
        joined = jnp.concatenate([act_one, act_dil], axis=1)
        merged = jnp.maximum(dot_f32(joined, whole_merge, 1, 0) + merge_bias, 0.0)
        merged = merged.astype(jnp.bfloat16)
        grad_out = jnp.where(merged > 0, flat_cotangent, jnp.zeros((), jnp.bfloat16))
        back = dot_f32(grad_out, whole_merge, 1, 1)
        kept = jnp.where(joined > 0, back, 0.0).astype(jnp.bfloat16)
        grad_dil = kept[:, branch:]
        centre_gradient = None

    def shifted_gradients(block):
        block = block.reshape(rows, width, branch)
        parts = [column_shifted(block, (1 - j) * DILATION_RATE) for j in range(3)]
        return [part.reshape(pixels, branch) for part in parts]

    if not paired:
        centre_gradient = jnp.concatenate([kept[:, :branch]] + shifted_gradients(grad_dil), axis=1)
    halos = [swapped(grad_dil, device_step, 0), swapped(grad_dil, device_step, 1)]
    if paired:
        own_merge, other_merge = merge_gradient(joined, grad_out, me)
    else:
        joined_relative = dot_f32(joined, merge_to_relative, 1, 0).astype(jnp.bfloat16)
        merge_total = dot_f32(joined_relative, grad_out, 0, 0)
        own_merge = merge_total[: joined_width // 2]
        other_merge = merge_total[joined_width // 2 :]
    merge_arrived = exchanged(other_merge, 0)

    centre_gradient, own_merge = together(centre_gradient, own_merge)
    own_total, other_total = [None] * 3, [None] * 3
    other_total[2] = dot_f32(flat_other, centre_gradient, 0, 0).astype(jnp.bfloat16)
    own_total[2] = dot_f32(flat_own, centre_gradient, 0, 0)
    *halos, own_total[2], other_total[2] = together(*halos, own_total[2], other_total[2])
    if paired:
        gradients = [*shifted(width, device_step, *halos, me), centre_gradient]
    else:
        halos = [jnp.where(upward, *halos), jnp.where(upward, *halos[::-1])]
        gradients = [jnp.concatenate(shifted_gradients(h), axis=1) for h in halos]
        gradients = together(*gradients) + [centre_gradient]
    for p in range(2):
        other_total[p] = dot_f32(flat_other, gradients[p], 0, 0).astype(jnp.bfloat16)
        own_total[p] = dot_f32(flat_own, gradients[p], 0, 0)
    if paired:
        sending = together(*other_total)
        arrived = together(*[exchanged(t, 0) for t in sending])
        own_blocks = device_count // 2
        owns = [x.reshape(own_blocks, -1, x.shape[-1]) for x in (*own_total, own_merge)]
        arrived = [x.reshape(own_blocks, -1, x.shape[-1]) for x in (*arrived, merge_arrived)]
        left = [list(range(bit_count - 1, 0, -1)) for _ in orders]
        for step in range(len(orders[0])):
            bits_now = [o[-1 - step] for o in orders]
            inners = [1 << (len(x) - 1 - x.index(b)) for x, b in zip(left, bits_now)]
            owns, sent = fold(owns, arrived, tables, inners)
            for x, b in zip(left, bits_now):
                x.remove(b)
            if step == 0:
                *sent, g0, g1, g2 = together(*sent, *gradients)
                input_grad = input_gradient([g0, g1, g2], own_weight, other_weight, me)
            else:
                sent = together(*sent)
            arrived = together(*[exchanged(t, b) for t, b in zip(sent, bits_now)])
            if step == 0:
                *arrived, input_grad = together(*arrived, input_grad)
        keep, sent = last_fold(owns, arrived)
        branch_kernel_gradient, grad_merge = scaled(
            keep,
            exchanged(sent, far_bits[0]),
            tables,
            scale,
            own_channels,
            joined_rows,
            merged_width,
        )
        branch_kernel_gradient = branch_kernel_gradient.transpose(1, 0, 2)
    else:
        merge_total = own_merge + merge_arrived.astype(jnp.float32)
        merge_total = merge_total.reshape((2,) * (bit_count - 1) + (joined_rows, merged_width))
        merge_parts = halves(merge_total, far_bits[0], bit_count) if far_bits else None
        sending = list(other_total) + ([merge_parts[1]] if far_bits else [])
        arrived = [
            exchanged(t, b) for t, b in zip(together(*sending), [0, 0, 0] + far_bits[:1])
        ]
        arrived = together(*arrived)
        if far_bits:
            merge_total = merge_parts[0] + arrived.pop().astype(jnp.float32)
        for bit in far_bits[1:]:
            own, other = halves(merge_total, bit, bit_count)
            merge_total = own + exchanged(other, bit).astype(jnp.float32)
        totals = []
        for own, a, o in zip(own_total, arrived, orders):
            shape = (2,) * (bit_count - 1) + (own.shape[0] // (device_count // 2), own.shape[1])
            totals.append(added(own.reshape(shape), a.reshape(shape), o[-1], bit_count))
        totals.append(halves(merge_total, crossing[3][-1], bit_count))
        *sent, g0, g1, g2 = together(*[t[1] for t in totals], *gradients)
        input_total = sum(
            dot_f32(g, jnp.concatenate([a, b], axis=0), 1, 1)
            for g, a, b in zip((g0, g1, g2), own_weight, other_weight)
        ).astype(jnp.bfloat16)
        input_grad = dot_f32(input_total, to_relative, 1, 1).astype(jnp.bfloat16)
        for step in range(len(orders[0])):
            arrived = together(*[exchanged(t, o[-1 - step]) for t, o in zip(sent, crossing)])
            if step == 0:
                *arrived, input_grad = together(*arrived, input_grad)
            own = [t[0] for t in totals]
            if step + 1 < len(orders[0]):
                totals = [
                    added(t, a, o[-2 - step], bit_count) for t, a, o in zip(own, arrived, crossing)
                ]
                sent = together(*[t[1] for t in totals])
            else:
                totals = [t + a.astype(jnp.float32) for t, a in zip(own, arrived)]
        grad_merge = totals[3].reshape(joined_rows, merged_width) * scale
        total = jnp.concatenate(totals[:3], axis=-1)
        for bit in far_bits[::-1]:
            own, other = halves(total, bit, bit_count)
            total = own + exchanged(other, bit).astype(jnp.float32)
        weight_gradient = dict(
            zip([k for p in PORTIONS for k in p], by_tap(total.reshape(own_channels, -1)))
        )
        branch_kernel_gradient = jnp.stack([weight_gradient[k] for k in range(taps)], axis=1) * scale

    return (
        merged.reshape(rows, width, merged_width),
        input_grad.reshape(rows, width, channels),
        branch_kernel_gradient,
        grad_merge,
    )


def solution(mesh):
    placed = (
        P(("grp", "row"), None, None),
        P("row", None, None),
        P(),
        P("row", None),
        P(),
        P(("grp", "row"), None, None),
    )
    return jax.shard_map(
        on_device,
        mesh=mesh,
        in_specs=placed,
        out_specs=(
            P(("grp", "row"), None, None),
            P(("grp", "row"), None, None),
            P(("grp", "row"), None, None),
            P(("grp", "row"), None),
        ),
        check_vma=False,
    )
```

```python
import functools
import math

import jax
import jax.numpy as jnp
from jax import lax
from jax.experimental import pallas as pl
from jax.experimental.pallas import tpu as pltpu
from jax.sharding import PartitionSpec as P

DILATION_RATE = 18
LANES = 128
PORTIONS = ((1, 2, 3), (7, 8, 9), (0, 4, 5, 6))


def swapped(block, distance, parity):
    count = lax.axis_size("row")
    pairs = [(i, i + distance) for i in range(count - distance) if i // distance % 2 == parity]
    return lax.ppermute(block, "row", pairs + [(b, a) for a, b in pairs])


def exchanged(block, bit):
    return lax.ppermute(block, "row", [(i, i ^ (1 << bit)) for i in range(lax.axis_size("row"))])


def dot_f32(left, right, left_dim, right_dim):
    return lax.dot_general(
        left, right, (((left_dim,), (right_dim,)), ((), ())), preferred_element_type=jnp.float32
    )


def bit_orders(bit_count):
    near = [b for b in (3, 2, 1) if b < bit_count]
    return [near[k:] + near[:k] for k in range(3)]


def axis_of(bit, bit_count):
    return bit_count - 1 - bit


def after(value, *others):
    return lax.optimization_barrier((value,) + others)[0]


def together(*values):
    return list(lax.optimization_barrier(values))


def gathered(blocks, crossed, bit_count):
    arrived = together(*[exchanged(b, bit) for b, bit in zip(blocks, crossed)])
    return [
        jnp.concatenate([b, a], axis=axis_of(bit, bit_count))
        for b, a, bit in zip(blocks, arrived, crossed)
    ]


def added(own, arrived, bit, bit_count):
    axis = axis_of(bit, bit_count)

    def half(k):
        parts = [lax.slice_in_dim(x, k, k + 1, axis=axis) for x in (own, arrived)]
        return parts[0] + parts[1].astype(jnp.float32)

    return half(0), half(1).astype(jnp.bfloat16)


def halves(block, bit, bit_count):
    axis = axis_of(bit, bit_count)
    return (
        lax.slice_in_dim(block, 0, 1, axis=axis),
        lax.slice_in_dim(block, 1, 2, axis=axis).astype(jnp.bfloat16),
    )


def relative_order(size, device_count, me):
    width = size // device_count
    target = lax.broadcasted_iota(jnp.int32, (size, size), 1)
    source = lax.broadcasted_iota(jnp.int32, (size, size), 0)
    half = device_count // 2
    block, inner = target // width, target % width
    device = (block % half) * 2 + block // half
    return (source == (device ^ me) * width + inner).astype(jnp.bfloat16)


def reorder_kernel(me_ref, x_ref, own_ref, other_ref):
    me = me_ref[0]
    chip, core = me // 2, me % 2
    lane = lax.broadcasted_iota(jnp.int32, (x_ref.shape[0], LANES), 1)
    low_lane = lane < LANES // 2

    def tile(block):
        start = pl.multiple_of((block ^ chip) * LANES, LANES)
        return x_ref[:, pl.ds(start, LANES)].astype(jnp.float32)

    for t in range(own_ref.shape[1] // LANES):
        first, second = tile(2 * t), tile(2 * t + 1)
        low = jnp.where(low_lane, first, pltpu.roll(second, LANES // 2, 1)).astype(jnp.bfloat16)
        high = jnp.where(low_lane, pltpu.roll(first, LANES // 2, 1), second).astype(jnp.bfloat16)
        columns = slice(t * LANES, (t + 1) * LANES)
        own_ref[:, columns] = jnp.where(core == 0, low, high)
        other_ref[:, columns] = jnp.where(core == 0, high, low)


def reordered(flat, me):
    pixels, channels = flat.shape
    half = jax.ShapeDtypeStruct((pixels, channels // 2), flat.dtype)
    return pl.pallas_call(
        reorder_kernel,
        out_shape=(half, half),
        in_specs=[
            pl.BlockSpec(memory_space=pltpu.SMEM),
            pl.BlockSpec(memory_space=pltpu.VMEM),
        ],
        out_specs=(pl.BlockSpec(memory_space=pltpu.VMEM),) * 2,
        cost_estimate=pl.CostEstimate(
            flops=8 * pixels * channels, bytes_accessed=4 * pixels * channels, transcendentals=0
        ),
        compiler_params=pltpu.CompilerParams(vmem_limit_bytes=12 << 20),
        name="reorder",
    )(me.reshape(1), flat)


def input_gradient_kernel(portion_count, me_ref, *refs):
    me = me_ref[0]
    chip, core = me // 2, me % 2
    gradients = refs[:portion_count]
    own, other = refs[portion_count : 2 * portion_count], refs[2 * portion_count : -1]
    out_ref = refs[-1]
    rows = LANES // 2

    def step(t, carry):
        total = None
        for p in range(portion_count):
            taken = []
            for k in range(2):
                at = pl.ds(pl.multiple_of(((2 * t + k) ^ chip) * rows, rows), rows)
                a, b = own[p][at, :], other[p][at, :]
                taken += [jnp.where(core == 0, a, b), jnp.where(core == 0, b, a)]
            part = dot_f32(gradients[p][...], jnp.concatenate(taken, axis=0), 1, 1)
            total = part if total is None else total + part
        columns = pl.ds(pl.multiple_of(t * 2 * LANES, 2 * LANES), 2 * LANES)
        out_ref[:, columns] = total.astype(out_ref.dtype)
        return carry

    lax.fori_loop(0, out_ref.shape[1] // (2 * LANES), step, 0, unroll=True)


def input_gradient(gradients, own, other, me):
    pixels = gradients[0].shape[0]
    half = own[0].shape[0]
    operands = [pltpu.with_memory_space_constraint(x, pltpu.VMEM) for x in (*gradients, *own, *other)]
    columns = sum(g.shape[1] for g in gradients)
    return pl.pallas_call(
        functools.partial(input_gradient_kernel, len(gradients)),
        out_shape=jax.ShapeDtypeStruct((pixels, 2 * half), jnp.bfloat16),
        in_specs=[pl.BlockSpec(memory_space=pltpu.SMEM)]
        + [pl.BlockSpec(memory_space=pltpu.VMEM)] * len(operands),
        out_specs=pl.BlockSpec(memory_space=pltpu.VMEM),
        cost_estimate=pl.CostEstimate(
            flops=4 * pixels * columns * half,
            bytes_accessed=2 * (pixels * columns + 2 * half * columns + 2 * pixels * half),
            transcendentals=0,
        ),
        compiler_params=pltpu.CompilerParams(vmem_limit_bytes=16 << 20),
        name="input_gradient",
    )(me.reshape(1), *operands)


def moved_rows(block, width, shift):
    if shift == 0:
        return block
    size = block.shape[0]
    column = lax.broadcasted_iota(jnp.int32, block.shape, 0) % width + shift
    inside = (column >= 0) & (column < width)
    return jnp.where(inside, pltpu.roll(block, (-shift) % size, 0), 0.0)


def head_kernel(
    width, centre_ref, above_ref, below_ref, bias_ref, merge_ref, merge_bias_ref, cotangent_ref,
    merged_ref, dilated_ref, gradient_ref, joined_ref, grad_out_ref,
):
    branch = above_ref.shape[1]
    z_dil = above_ref[...] + below_ref[...]
    for j in range(3):
        part = centre_ref[:, (1 + j) * branch : (2 + j) * branch]
        z_dil = z_dil + moved_rows(part, width, (j - 1) * DILATION_RATE)
    act_one = jnp.maximum(centre_ref[:, :branch] + bias_ref[0:1, :], 0.0).astype(jnp.bfloat16)
    act_dil = jnp.maximum(z_dil + bias_ref[1:2, :], 0.0).astype(jnp.bfloat16)
    joined = jnp.concatenate([act_one, act_dil], axis=1)
    joined_ref[...] = joined
    merged = jnp.maximum(dot_f32(joined, merge_ref[...], 1, 0) + merge_bias_ref[...], 0.0)
    merged = merged.astype(jnp.bfloat16)
    merged_ref[...] = merged
    cotangent = cotangent_ref[...].astype(jnp.float32)
    grad_out = jnp.where(merged.astype(jnp.float32) > 0, cotangent, 0.0).astype(jnp.bfloat16)
    grad_out_ref[...] = grad_out
    back = dot_f32(grad_out, merge_ref[...], 1, 1)
    kept = jnp.where(joined.astype(jnp.float32) > 0, back, 0.0).astype(jnp.bfloat16)
    dilated = kept[:, branch:]
    dilated_ref[...] = dilated
    gradient_ref[:, :branch] = kept[:, :branch]
    for j in range(3):
        moved = moved_rows(dilated.astype(jnp.float32), width, (1 - j) * DILATION_RATE)
        gradient_ref[:, (1 + j) * branch : (2 + j) * branch] = moved.astype(jnp.bfloat16)


def head(width, centre, above, below, bias, whole_merge, merge_bias, cotangent):
    pixels, branch = above.shape
    merged_width = whole_merge.shape[1]
    widths = (merged_width, branch, 4 * branch, 2 * branch, merged_width)
    operands = (centre, above, below, bias, whole_merge, merge_bias.reshape(1, -1), cotangent)
    return pl.pallas_call(
        functools.partial(head_kernel, width),
        out_shape=[jax.ShapeDtypeStruct((pixels, w), jnp.bfloat16) for w in widths],
        in_specs=[pl.BlockSpec(memory_space=pltpu.VMEM)] * len(operands),
        out_specs=[pl.BlockSpec(memory_space=pltpu.VMEM)] * len(widths),
        cost_estimate=pl.CostEstimate(
            flops=8 * pixels * branch * merged_width,
            bytes_accessed=8 * pixels * (6 * branch + merged_width),
            transcendentals=0,
        ),
        compiler_params=pltpu.CompilerParams(vmem_limit_bytes=12 << 20),
        name="head",
    )(*operands)


def is_upward(me, step):
    return me // step % 2 == 0


def halo_kernel(width, step, me_ref, first_ref, second_ref, first_out_ref, second_out_ref):
    branch = first_out_ref.shape[1]
    sums = []
    for ref in (first_ref, second_ref):
        total = None
        for j in range(3):
            part = ref[:, j * branch : (j + 1) * branch]
            moved = moved_rows(part, width, (j - 1) * DILATION_RATE)
            total = moved if total is None else total + moved
        sums.append(total)
    upward = is_upward(me_ref[0], step)
    first_out_ref[...] = jnp.where(upward, sums[0], sums[1])
    second_out_ref[...] = jnp.where(upward, sums[1], sums[0])


def halo_sums(width, step, products, me):
    pixels, taps = products[0].shape
    out = jax.ShapeDtypeStruct((pixels, taps // 3), jnp.float32)
    return halo_call(functools.partial(halo_kernel, width, step), "halo_sums", out, me, *products)


def shift_kernel(width, step, flip, me_ref, first_ref, second_ref, first_out_ref, second_out_ref):
    branch = first_ref.shape[1]
    upward = is_upward(me_ref[0] ^ flip, step)
    first, second = first_ref[...].astype(jnp.float32), second_ref[...].astype(jnp.float32)
    pairs = ((first, second, first_out_ref), (second, first, second_out_ref))
    for here, there, out_ref in pairs:
        block = jnp.where(upward, here, there)
        for j in range(3):
            moved = moved_rows(block, width, (1 - j) * DILATION_RATE)
            out_ref[:, j * branch : (j + 1) * branch] = moved.astype(jnp.bfloat16)


def shifted(width, step, first, second, me, flip=0):
    pixels, branch = first.shape
    out = jax.ShapeDtypeStruct((pixels, 3 * branch), jnp.bfloat16)
    kernel = functools.partial(shift_kernel, width, step, flip)
    return halo_call(kernel, "shift", out, me, first, second)


def halo_call(kernel, name, out, me, first, second):
    return pl.pallas_call(
        kernel,
        out_shape=(out, out),
        in_specs=[pl.BlockSpec(memory_space=pltpu.SMEM)]
        + [pl.BlockSpec(memory_space=pltpu.VMEM)] * 2,
        out_specs=(pl.BlockSpec(memory_space=pltpu.VMEM),) * 2,
        cost_estimate=pl.CostEstimate(
            flops=0, bytes_accessed=8 * (first.size + out.size), transcendentals=0
        ),
        compiler_params=pltpu.CompilerParams(vmem_limit_bytes=8 << 20),
        name=name,
    )(me.reshape(1), first, second)


def merge_gradient_kernel(me_ref, joined_ref, grad_out_ref, own_ref, other_ref, total_ref):
    me = me_ref[0]
    total_ref[...] = dot_f32(joined_ref[...], grad_out_ref[...], 0, 0)
    half = own_ref.shape[0]
    group = 8
    for k in range(half // group):
        here = slice(k * group, (k + 1) * group)
        device = (2 * k) ^ me
        own_ref[here, :] = total_ref[pl.ds(pl.multiple_of(device * group, group), group), :]
        device = (2 * k + 1) ^ me
        other_ref[here, :] = total_ref[pl.ds(pl.multiple_of(device * group, group), group), :]


def merge_gradient(joined, grad_out, me):
    pixels, width = joined.shape
    half = jax.ShapeDtypeStruct((width // 2, grad_out.shape[1]), jnp.float32)
    return pl.pallas_call(
        merge_gradient_kernel,
        out_shape=(half, half),
        in_specs=[pl.BlockSpec(memory_space=pltpu.SMEM)]
        + [pl.BlockSpec(memory_space=pltpu.VMEM)] * 2,
        out_specs=(pl.BlockSpec(memory_space=pltpu.VMEM),) * 2,
        scratch_shapes=[pltpu.VMEM((width, grad_out.shape[1]), jnp.float32)],
        cost_estimate=pl.CostEstimate(
            flops=2 * pixels * width * grad_out.shape[1],
            bytes_accessed=8 * pixels * width,
            transcendentals=0,
        ),
        compiler_params=pltpu.CompilerParams(vmem_limit_bytes=8 << 20),
        name="merge_gradient",
    )(me.reshape(1), joined, grad_out)


def layout(rows, merge_rows, merge_width):
    shares = (0, rows // 4, rows // 2, rows)
    tables = []
    for p, portion in enumerate(PORTIONS):
        table = [(k, 0, n * rows, rows) for n, k in enumerate(k for k in portion if k > 0)]
        table.append((0, shares[p], 3 * rows, shares[p + 1] - shares[p]))
        if p == 2:
            first = 3 * rows + table[-1][3]
            lanes = range(0, merge_width, LANES)
            table += [(None, x, first + n * merge_rows, merge_rows) for n, x in enumerate(lanes)]
        tables.append(table)
    return tables


def stack_rows(table):
    return table[-1][2] + table[-1][3]


def lanes_of(k):
    for p, portion in enumerate(PORTIONS):
        if k in portion:
            at = portion.index(k) * LANES
            return p, slice(at, at + LANES)


def local_call(kernel, name, out_shape, operands, moved, grant):
    return pl.pallas_call(
        kernel,
        out_shape=out_shape,
        in_specs=[pl.BlockSpec(memory_space=pltpu.VMEM)] * len(operands),
        out_specs=[pl.BlockSpec(memory_space=pltpu.VMEM)] * len(out_shape),
        cost_estimate=pl.CostEstimate(flops=moved // 4, bytes_accessed=moved, transcendentals=0),
        compiler_params=pltpu.CompilerParams(vmem_limit_bytes=grant << 20),
        name=name,
    )(*operands)


def pack_kernel(tables, weight_ref, merge_ref, out_ref, sems):
    copies, base = [], 0
    for table in tables:
        for k, there, here, count in table:
            if k is None:
                source = merge_ref.at[:, pl.ds(there, LANES)]
            else:
                source = weight_ref.at[k, pl.ds(there, count), :]
            target = out_ref.at[pl.ds(base + here, count), :]
            copies.append(pltpu.make_async_copy(source, target, sems.at[len(copies)]))
        base += stack_rows(table)
    for copy in copies:
        copy.start()
    for copy in copies:
        copy.wait()


def pack(weight, merge_weight, tables):
    return pl.pallas_call(
        functools.partial(pack_kernel, tables),
        out_shape=jax.ShapeDtypeStruct((sum(map(stack_rows, tables)), LANES), weight.dtype),
        in_specs=[pl.BlockSpec(memory_space=pltpu.HBM)] * 2,
        out_specs=pl.BlockSpec(memory_space=pltpu.VMEM),
        scratch_shapes=[pltpu.SemaphoreType.DMA((sum(map(len, tables)),))],
        cost_estimate=pl.CostEstimate(flops=0, bytes_accessed=4 * weight.size, transcendentals=0),
        compiler_params=pltpu.CompilerParams(vmem_limit_bytes=4 << 20),
        name="pack",
    )(*(pltpu.with_memory_space_constraint(x, pltpu.HBM) for x in (weight, merge_weight)))


def block_pair(target, inner):
    low = target // inner * (2 * inner) + target % inner
    return low, low + inner


def unpack_kernel(tables, inners, *refs):
    outs = refs[6:]

    def step(target, carry):
        for p, table in enumerate(tables):
            for ref, block in zip(refs[2 * p : 2 * p + 2], block_pair(target, inners[p])):
                for k, there, here, count in table:
                    value = ref[target, here : here + count, :]
                    if k is None:
                        outs[3][block, :, there : there + LANES] = value
                    else:
                        q, lanes = lanes_of(k)
                        outs[q][block, there : there + count, lanes] = value
        return carry

    lax.fori_loop(0, refs[0].shape[0], step, 0)


def unpack(pairs, tables, inners, rows, merge_rows, merge_width):
    blocks = 2 * pairs[0].shape[0]
    shapes = [(blocks, rows, LANES * len(p)) for p in PORTIONS] + [(blocks, merge_rows, merge_width)]
    out = [jax.ShapeDtypeStruct(x, jnp.bfloat16) for x in shapes]
    kernel = functools.partial(unpack_kernel, tables, tuple(inners))
    return local_call(kernel, "unpack", out, pairs, 4 * sum(x.size for x in pairs), 16)


def first_fold_kernel(tables, inners, *refs):
    owns, arrived, keeps, sends = refs[:4], refs[4], refs[5:8], refs[8:]

    def step(target, carry):
        for p, table in enumerate(tables):
            for half, block in enumerate(block_pair(target, inners[p])):
                for k, there, here, count in table:
                    if k is None:
                        q, at = 3, (block, slice(None), slice(there, there + LANES))
                    else:
                        q, lanes = lanes_of(k)
                        at = (block, slice(there, there + count), lanes)
                    value = owns[q][at]
                    if k is None:
                        value = value + arrived[at]
                    out_ref = (keeps, sends)[half][p]
                    out_ref[target, here : here + count, :] = value.astype(out_ref.dtype)
        return carry

    lax.fori_loop(0, keeps[0].shape[0], step, 0)


def fold_kernel(inners, *refs):
    owns, arriveds, keeps, sends = (refs[3 * k : 3 * k + 3] for k in range(4))

    def step(target, carry):
        for p in range(3):
            for half, block in enumerate(block_pair(target, inners[p])):
                value = owns[p][block] + arriveds[p][block].astype(jnp.float32)
                out_ref = (keeps, sends)[half][p]
                out_ref[target] = value.astype(out_ref.dtype)
        return carry

    lax.fori_loop(0, keeps[0].shape[0], step, 0)


def fold(owns, arriveds, tables, inners):
    shapes = [(owns[0].shape[0] // 2, stack_rows(table), LANES) for table in tables]
    out = [jax.ShapeDtypeStruct(x, t) for t in (jnp.float32, jnp.bfloat16) for x in shapes]
    if len(owns) == 4:
        kernel = functools.partial(first_fold_kernel, tables, tuple(inners))
    else:
        kernel = functools.partial(fold_kernel, tuple(inners))
    moved = 9 * sum(x.size for x in owns)
    out = local_call(kernel, "fold", out, (*owns, *arriveds), moved, 20)
    return out[:3], out[3:]


def last_fold_kernel(*refs):
    owns, arriveds = refs[:3], refs[3:6]
    base = 0
    for own, arrived in zip(owns, arriveds):
        at = slice(base, base + own.shape[1])
        base += own.shape[1]
        refs[6][at, :] = own[0] + arrived[0].astype(jnp.float32)
        refs[7][at, :] = (own[1] + arrived[1].astype(jnp.float32)).astype(jnp.bfloat16)


def last_fold(owns, arriveds):
    shape = (sum(x.shape[1] for x in owns), LANES)
    out = [jax.ShapeDtypeStruct(shape, t) for t in (jnp.float32, jnp.bfloat16)]
    moved = 9 * sum(x.size for x in owns)
    return local_call(last_fold_kernel, "last_fold", out, (*owns, *arriveds), moved, 8)


def scaled_kernel(tables, scale, keep_ref, arrived_ref, out_ref, out_merge_ref):
    base = 0
    for table in tables:
        for k, there, here, count in table:
            at = slice(base + here, base + here + count)
            value = (keep_ref[at, :] + arrived_ref[at, :].astype(jnp.float32)) * scale
            if k is None:
                out_merge_ref[:, there : there + LANES] = value
            else:
                out_ref[k, there : there + count, :] = value
        base += stack_rows(table)


def scaled(keep, arrived, tables, scale, rows, merge_rows, merge_width):
    taps = sum(map(len, PORTIONS))
    out = [
        jax.ShapeDtypeStruct((taps, rows, LANES), jnp.float32),
        jax.ShapeDtypeStruct((merge_rows, merge_width), jnp.float32),
    ]
    kernel = functools.partial(scaled_kernel, tables, scale)
    return local_call(kernel, "scaled", out, (keep, arrived), 10 * keep.size, 8)


def column_shifted(rows, shift):
    width = rows.shape[1]
    if shift == 0:
        return rows
    if shift > 0:
        return jnp.pad(rows[:, shift:], ((0, 0), (0, shift), (0, 0)))
    return jnp.pad(rows[:, : width + shift], ((0, 0), (-shift, 0), (0, 0)))


def on_device(
    features, branch_kernel_weight, branch_norm_bias, merge_weight, merge_bias, cotangent
):
    device_count = lax.axis_size("row")
    bit_count = device_count.bit_length() - 1
    me = lax.axis_index("row")
    rows, width, channels = features.shape
    taps, branch = branch_kernel_weight.shape[1:]
    own_channels = branch_kernel_weight.shape[0]
    joined_rows, merged_width = merge_weight.shape
    joined_width = joined_rows * device_count
    pixels = rows * width
    scale = 1.0 / math.sqrt(rows * device_count * width)
    device_step = DILATION_RATE // rows
    bits = (1,) * (bit_count - 1)
    orders = bit_orders(bit_count)
    far_bits = list(range(bit_count - 1, 3, -1))
    paired = 2 * own_channels == LANES and joined_rows == 8 and branch == LANES and bit_count == 5
    portion_widths = [len(p) * branch for p in PORTIONS]

    def split(array, widths):
        starts = [sum(widths[:i]) for i in range(len(widths))]
        return [lax.slice_in_dim(array, s, s + w, axis=-1) for s, w in zip(starts, widths)]

    tap_order = [k for portion in PORTIONS for k in portion]
    weight = branch_kernel_weight.transpose(1, 0, 2)
    half_rows = channels // 2
    crossing = orders + [orders[1]]
    flat = features.reshape(pixels, channels)
    if paired:
        tables = layout(own_channels, joined_rows, merged_width)
        block = pack(weight, merge_weight, tables)
        block, flat, me = together(block, flat, me)
        flat_own, flat_other = reordered(flat, me)
        block = block.reshape(bits + block.shape)
        (arrived,) = together(exchanged(block, far_bits[0]))
        block, arrived, flat_own, flat_other = together(block, arrived, flat_own, flat_other)
        blocks, base = [], 0
        for table in tables:
            parts = [
                lax.slice_in_dim(x, base, base + stack_rows(table), axis=-2) for x in (block, arrived)
            ]
            blocks.append(jnp.concatenate(parts, axis=0))
            base += stack_rows(table)
        for step in range(len(orders[0]) - 1):
            blocks = gathered(together(*blocks), [o[step] for o in orders], bit_count)
        blocks = together(*blocks)
        arrived = together(*[exchanged(b, o[-1]) for b, o in zip(blocks, orders)])
        pairs = [
            x.reshape((device_count // 4,) + x.shape[-2:])
            for pair in zip(blocks, arrived)
            for x in pair
        ]
        inners = [1 << (o[-1] - 1) for o in orders]
        *own_weight, own_merge = unpack(
            pairs, tables, inners, own_channels, joined_rows, merged_width
        )
        own_weight = [x.reshape(half_rows, x.shape[-1]) for x in own_weight]
    else:
        block = jnp.concatenate([weight[k] for k in tap_order], axis=1)
        to_relative = relative_order(channels, device_count, me)
        flat = dot_f32(flat, to_relative, 1, 0).astype(jnp.bfloat16)
        flat_own, flat_other = flat[:, :half_rows], flat[:, half_rows:]
        block = block.reshape(bits + block.shape)
        merge_block = merge_weight.reshape(bits + merge_weight.shape)
        for bit in far_bits:
            block, merge_block = gathered([block, merge_block], [bit, bit], bit_count)
        blocks = split(block, portion_widths) + [merge_block]
        for step in range(len(orders[0])):
            blocks = gathered(together(*blocks), [o[step] for o in crossing], bit_count)
        own_merge = blocks.pop()
        own_weight = [b.reshape(half_rows, b.shape[-1]) for b in blocks]
    own_merge = own_merge.reshape(joined_width // 2, merged_width)

    def row_sum(parts):
        total = None
        for j, part in enumerate(parts):
            moved = column_shifted(part.reshape(rows, width, branch), (j - 1) * DILATION_RATE)
            total = moved if total is None else total + moved
        return total

    def by_tap(product):
        return split(product, [branch] * (product.shape[1] // branch))

    other_weight = [exchanged(w, 0) for w in own_weight[:2]]
    sums = [dot_f32(flat_own, w, 1, 0) for w in own_weight[:2]]
    other_weight[0], *sums = together(other_weight[0], *sums)
    sums = [x + dot_f32(flat_other, w, 1, 0) for x, w in zip(sums, other_weight)]
    upward = is_upward(me, device_step)
    if paired:
        sums = halo_sums(width, device_step, sums, me)
    else:
        sums = [row_sum(by_tap(x)).reshape(pixels, branch) for x in sums]
        sums = [jnp.where(upward, *sums), jnp.where(upward, *sums[::-1])]
    merge_to_relative = relative_order(joined_width, device_count, me)
    own_weight[2], own_merge, *sums = together(own_weight[2], own_merge, *sums)
    whole_merge = dot_f32(
        merge_to_relative, jnp.concatenate([own_merge, exchanged(own_merge, 0)], axis=0), 1, 0
    ).astype(jnp.bfloat16)
    other_weight.append(exchanged(own_weight[2], 0))
    centre = dot_f32(flat_own, own_weight[2], 1, 0) + dot_f32(flat_other, other_weight[2], 1, 0)
    above, below = swapped(sums[0], device_step, 0), swapped(sums[1], device_step, 1)
    flat_cotangent = cotangent.reshape(pixels, merged_width)
    if paired:
        merged, grad_dil, centre_gradient, joined, grad_out = head(
            width, centre, above, below, branch_norm_bias, whole_merge, merge_bias, flat_cotangent
        )
    else:
        centre = by_tap(centre)
        z_dil = row_sum(centre[1:]).reshape(pixels, branch) + above + below
        act_one = jnp.maximum(centre[0] + branch_norm_bias[0], 0.0).astype(jnp.bfloat16)
        act_dil = jnp.maximum(z_dil + branch_norm_bias[1], 0.0).astype(jnp.bfloat16)
        joined = jnp.concatenate([act_one, act_dil], axis=1)
        merged = jnp.maximum(dot_f32(joined, whole_merge, 1, 0) + merge_bias, 0.0)
        merged = merged.astype(jnp.bfloat16)
        grad_out = jnp.where(merged > 0, flat_cotangent, jnp.zeros((), jnp.bfloat16))
        back = dot_f32(grad_out, whole_merge, 1, 1)
        kept = jnp.where(joined > 0, back, 0.0).astype(jnp.bfloat16)
        grad_dil = kept[:, branch:]
        centre_gradient = None

    def shifted_gradients(block):
        block = block.reshape(rows, width, branch)
        parts = [column_shifted(block, (1 - j) * DILATION_RATE) for j in range(3)]
        return [part.reshape(pixels, branch) for part in parts]

    if not paired:
        centre_gradient = jnp.concatenate([kept[:, :branch]] + shifted_gradients(grad_dil), axis=1)
    halos = [swapped(grad_dil, device_step, 0), swapped(grad_dil, device_step, 1)]
    if paired:
        own_merge, other_merge = merge_gradient(joined, grad_out, me)
    else:
        joined_relative = dot_f32(joined, merge_to_relative, 1, 0).astype(jnp.bfloat16)
        merge_total = dot_f32(joined_relative, grad_out, 0, 0)
        own_merge = merge_total[: joined_width // 2]
        other_merge = merge_total[joined_width // 2 :]
    merge_arrived = exchanged(other_merge, 0)

    centre_gradient, own_merge = together(centre_gradient, own_merge)
    own_total, other_total = [None] * 3, [None] * 3
    own_total[2] = dot_f32(flat_own, centre_gradient, 0, 0)
    if paired:
        flat_partner = exchanged(flat_other, 0)
        partner_gradient = exchanged(centre_gradient, 0)
        own_total[2] = own_total[2] + dot_f32(flat_partner, partner_gradient, 0, 0)
        *halos, own_total[2] = together(*halos, own_total[2])
        partner_halos = [exchanged(h, 0) for h in halos]
        gradients = [*shifted(width, device_step, *halos, me), centre_gradient]
        own_total[:2] = [dot_f32(flat_own, g, 0, 0) for g in gradients[:2]]
        *partner_halos, own_total[0], own_total[1] = together(*partner_halos, *own_total[:2])
        partner_gradients = shifted(width, device_step, *partner_halos, me, 1)
        for p in range(2):
            own_total[p] = own_total[p] + dot_f32(flat_partner, partner_gradients[p], 0, 0)
    else:
        other_total[2] = dot_f32(flat_other, centre_gradient, 0, 0).astype(jnp.bfloat16)
        *halos, own_total[2], other_total[2] = together(*halos, own_total[2], other_total[2])
        halos = [jnp.where(upward, *halos), jnp.where(upward, *halos[::-1])]
        gradients = [jnp.concatenate(shifted_gradients(h), axis=1) for h in halos]
        gradients = together(*gradients) + [centre_gradient]
        for p in range(2):
            other_total[p] = dot_f32(flat_other, gradients[p], 0, 0).astype(jnp.bfloat16)
            own_total[p] = dot_f32(flat_own, gradients[p], 0, 0)
    if paired:
        own_blocks = device_count // 2
        owns = [x.reshape(own_blocks, -1, x.shape[-1]) for x in (*own_total, own_merge)]
        arrived = [merge_arrived.reshape(owns[3].shape)]
        left = [list(range(bit_count - 1, 0, -1)) for _ in orders]
        for step in range(len(orders[0])):
            bits_now = [o[-1 - step] for o in orders]
            inners = [1 << (len(x) - 1 - x.index(b)) for x, b in zip(left, bits_now)]
            owns, sent = fold(owns, arrived, tables, inners)
            for x, b in zip(left, bits_now):
                x.remove(b)
            if step == 0:
                *sent, g0, g1, g2 = together(*sent, *gradients)
                input_grad = input_gradient([g0, g1, g2], own_weight, other_weight, me)
            else:
                sent = together(*sent)
            arrived = together(*[exchanged(t, b) for t, b in zip(sent, bits_now)])
            if step == 0:
                *arrived, input_grad = together(*arrived, input_grad)
        keep, sent = last_fold(owns, arrived)
        branch_kernel_gradient, grad_merge = scaled(
            keep,
            exchanged(sent, far_bits[0]),
            tables,
            scale,
            own_channels,
            joined_rows,
            merged_width,
        )
        branch_kernel_gradient = branch_kernel_gradient.transpose(1, 0, 2)
    else:
        merge_total = own_merge + merge_arrived.astype(jnp.float32)
        merge_total = merge_total.reshape((2,) * (bit_count - 1) + (joined_rows, merged_width))
        merge_parts = halves(merge_total, far_bits[0], bit_count) if far_bits else None
        sending = list(other_total) + ([merge_parts[1]] if far_bits else [])
        arrived = [
            exchanged(t, b) for t, b in zip(together(*sending), [0, 0, 0] + far_bits[:1])
        ]
        arrived = together(*arrived)
        if far_bits:
            merge_total = merge_parts[0] + arrived.pop().astype(jnp.float32)
        for bit in far_bits[1:]:
            own, other = halves(merge_total, bit, bit_count)
            merge_total = own + exchanged(other, bit).astype(jnp.float32)
        totals = []
        for own, a, o in zip(own_total, arrived, orders):
            shape = (2,) * (bit_count - 1) + (own.shape[0] // (device_count // 2), own.shape[1])
            totals.append(added(own.reshape(shape), a.reshape(shape), o[-1], bit_count))
        totals.append(halves(merge_total, crossing[3][-1], bit_count))
        *sent, g0, g1, g2 = together(*[t[1] for t in totals], *gradients)
        input_total = sum(
            dot_f32(g, jnp.concatenate([a, b], axis=0), 1, 1)
            for g, a, b in zip((g0, g1, g2), own_weight, other_weight)
        ).astype(jnp.bfloat16)
        input_grad = dot_f32(input_total, to_relative, 1, 1).astype(jnp.bfloat16)
        for step in range(len(orders[0])):
            arrived = together(*[exchanged(t, o[-1 - step]) for t, o in zip(sent, crossing)])
            if step == 0:
                *arrived, input_grad = together(*arrived, input_grad)
            own = [t[0] for t in totals]
            if step + 1 < len(orders[0]):
                totals = [
                    added(t, a, o[-2 - step], bit_count) for t, a, o in zip(own, arrived, crossing)
                ]
                sent = together(*[t[1] for t in totals])
            else:
                totals = [t + a.astype(jnp.float32) for t, a in zip(own, arrived)]
        grad_merge = totals[3].reshape(joined_rows, merged_width) * scale
        total = jnp.concatenate(totals[:3], axis=-1)
        for bit in far_bits[::-1]:
            own, other = halves(total, bit, bit_count)
            total = own + exchanged(other, bit).astype(jnp.float32)
        weight_gradient = dict(
            zip([k for p in PORTIONS for k in p], by_tap(total.reshape(own_channels, -1)))
        )
        branch_kernel_gradient = jnp.stack([weight_gradient[k] for k in range(taps)], axis=1) * scale

    return (
        merged.reshape(rows, width, merged_width),
        input_grad.reshape(rows, width, channels),
        branch_kernel_gradient,
        grad_merge,
    )


def solution(mesh):
    placed = (
        P(("grp", "row"), None, None),
        P("row", None, None),
        P(),
        P("row", None),
        P(),
        P(("grp", "row"), None, None),
    )
    return jax.shard_map(
        on_device,
        mesh=mesh,
        in_specs=placed,
        out_specs=(
            P(("grp", "row"), None, None),
            P(("grp", "row"), None, None),
            P(("grp", "row"), None, None),
            P(("grp", "row"), None),
        ),
        check_vma=False,
    )
```

```python
import functools
import math

import jax
import jax.numpy as jnp
from jax import lax
from jax.experimental import pallas as pl
from jax.experimental.pallas import tpu as pltpu
from jax.sharding import PartitionSpec as P

DILATION_RATE = 18
LANES = 128
PORTIONS = ((1, 2, 3), (7, 8, 9), (0, 4, 5, 6))


def swapped(block, distance, parity):
    count = lax.axis_size("row")
    pairs = [(i, i + distance) for i in range(count - distance) if i // distance % 2 == parity]
    return lax.ppermute(block, "row", pairs + [(b, a) for a, b in pairs])


def exchanged(block, bit):
    return lax.ppermute(block, "row", [(i, i ^ (1 << bit)) for i in range(lax.axis_size("row"))])


def dot_f32(left, right, left_dim, right_dim):
    return lax.dot_general(
        left, right, (((left_dim,), (right_dim,)), ((), ())), preferred_element_type=jnp.float32
    )


def bit_orders(bit_count):
    near = [b for b in (3, 2, 1) if b < bit_count]
    return [near[k:] + near[:k] for k in range(3)]


def axis_of(bit, bit_count):
    return bit_count - 1 - bit


def after(value, *others):
    return lax.optimization_barrier((value,) + others)[0]


def together(*values):
    return list(lax.optimization_barrier(values))


def gathered(blocks, crossed, bit_count):
    arrived = together(*[exchanged(b, bit) for b, bit in zip(blocks, crossed)])
    return [
        jnp.concatenate([b, a], axis=axis_of(bit, bit_count))
        for b, a, bit in zip(blocks, arrived, crossed)
    ]


def added(own, arrived, bit, bit_count):
    axis = axis_of(bit, bit_count)

    def half(k):
        parts = [lax.slice_in_dim(x, k, k + 1, axis=axis) for x in (own, arrived)]
        return parts[0] + parts[1].astype(jnp.float32)

    return half(0), half(1).astype(jnp.bfloat16)


def halves(block, bit, bit_count):
    axis = axis_of(bit, bit_count)
    return (
        lax.slice_in_dim(block, 0, 1, axis=axis),
        lax.slice_in_dim(block, 1, 2, axis=axis).astype(jnp.bfloat16),
    )


def relative_order(size, device_count, me):
    width = size // device_count
    target = lax.broadcasted_iota(jnp.int32, (size, size), 1)
    source = lax.broadcasted_iota(jnp.int32, (size, size), 0)
    half = device_count // 2
    block, inner = target // width, target % width
    device = (block % half) * 2 + block // half
    return (source == (device ^ me) * width + inner).astype(jnp.bfloat16)


def reorder_kernel(me_ref, x_ref, own_ref, other_ref):
    me = me_ref[0]
    chip, core = me // 2, me % 2
    lane = lax.broadcasted_iota(jnp.int32, (x_ref.shape[0], LANES), 1)
    low_lane = lane < LANES // 2

    def tile(block):
        start = pl.multiple_of((block ^ chip) * LANES, LANES)
        return x_ref[:, pl.ds(start, LANES)].astype(jnp.float32)

    for t in range(own_ref.shape[1] // LANES):
        first, second = tile(2 * t), tile(2 * t + 1)
        low = jnp.where(low_lane, first, pltpu.roll(second, LANES // 2, 1)).astype(jnp.bfloat16)
        high = jnp.where(low_lane, pltpu.roll(first, LANES // 2, 1), second).astype(jnp.bfloat16)
        columns = slice(t * LANES, (t + 1) * LANES)
        own_ref[:, columns] = jnp.where(core == 0, low, high)
        other_ref[:, columns] = jnp.where(core == 0, high, low)


def reordered(flat, me):
    pixels, channels = flat.shape
    half = jax.ShapeDtypeStruct((pixels, channels // 2), flat.dtype)
    return pl.pallas_call(
        reorder_kernel,
        out_shape=(half, half),
        in_specs=[
            pl.BlockSpec(memory_space=pltpu.SMEM),
            pl.BlockSpec(memory_space=pltpu.VMEM),
        ],
        out_specs=(pl.BlockSpec(memory_space=pltpu.VMEM),) * 2,
        cost_estimate=pl.CostEstimate(
            flops=8 * pixels * channels, bytes_accessed=4 * pixels * channels, transcendentals=0
        ),
        compiler_params=pltpu.CompilerParams(vmem_limit_bytes=12 << 20),
        name="reorder",
    )(me.reshape(1), flat)


def input_gradient_kernel(portion_count, me_ref, *refs):
    me = me_ref[0]
    chip, core = me // 2, me % 2
    gradients = refs[:portion_count]
    own, other = refs[portion_count : 2 * portion_count], refs[2 * portion_count : -1]
    out_ref = refs[-1]
    rows = LANES // 2

    def step(t, carry):
        total = None
        for p in range(portion_count):
            taken = []
            for k in range(2):
                at = pl.ds(pl.multiple_of(((2 * t + k) ^ chip) * rows, rows), rows)
                a, b = own[p][at, :], other[p][at, :]
                taken += [jnp.where(core == 0, a, b), jnp.where(core == 0, b, a)]
            part = dot_f32(gradients[p][...], jnp.concatenate(taken, axis=0), 1, 1)
            total = part if total is None else total + part
        columns = pl.ds(pl.multiple_of(t * 2 * LANES, 2 * LANES), 2 * LANES)
        out_ref[:, columns] = total.astype(out_ref.dtype)
        return carry

    lax.fori_loop(0, out_ref.shape[1] // (2 * LANES), step, 0, unroll=True)


def input_gradient(gradients, own, other, me):
    pixels = gradients[0].shape[0]
    half = own[0].shape[0]
    operands = [pltpu.with_memory_space_constraint(x, pltpu.VMEM) for x in (*gradients, *own, *other)]
    columns = sum(g.shape[1] for g in gradients)
    return pl.pallas_call(
        functools.partial(input_gradient_kernel, len(gradients)),
        out_shape=jax.ShapeDtypeStruct((pixels, 2 * half), jnp.bfloat16),
        in_specs=[pl.BlockSpec(memory_space=pltpu.SMEM)]
        + [pl.BlockSpec(memory_space=pltpu.VMEM)] * len(operands),
        out_specs=pl.BlockSpec(memory_space=pltpu.VMEM),
        cost_estimate=pl.CostEstimate(
            flops=4 * pixels * columns * half,
            bytes_accessed=2 * (pixels * columns + 2 * half * columns + 2 * pixels * half),
            transcendentals=0,
        ),
        compiler_params=pltpu.CompilerParams(vmem_limit_bytes=16 << 20),
        name="input_gradient",
    )(me.reshape(1), *operands)


def moved_rows(block, width, shift):
    if shift == 0:
        return block
    size = block.shape[0]
    column = lax.broadcasted_iota(jnp.int32, block.shape, 0) % width + shift
    inside = (column >= 0) & (column < width)
    return jnp.where(inside, pltpu.roll(block, (-shift) % size, 0), 0.0)


def head_kernel(
    width, centre_ref, above_ref, below_ref, bias_ref, merge_ref, merge_bias_ref, cotangent_ref,
    merged_ref, dilated_ref, gradient_ref, joined_ref, grad_out_ref,
):
    branch = above_ref.shape[1]
    z_dil = above_ref[...] + below_ref[...]
    for j in range(3):
        part = centre_ref[:, (1 + j) * branch : (2 + j) * branch]
        z_dil = z_dil + moved_rows(part, width, (j - 1) * DILATION_RATE)
    act_one = jnp.maximum(centre_ref[:, :branch] + bias_ref[0:1, :], 0.0).astype(jnp.bfloat16)
    act_dil = jnp.maximum(z_dil + bias_ref[1:2, :], 0.0).astype(jnp.bfloat16)
    joined = jnp.concatenate([act_one, act_dil], axis=1)
    joined_ref[...] = joined
    merged = jnp.maximum(dot_f32(joined, merge_ref[...], 1, 0) + merge_bias_ref[...], 0.0)
    merged = merged.astype(jnp.bfloat16)
    merged_ref[...] = merged
    cotangent = cotangent_ref[...].astype(jnp.float32)
    grad_out = jnp.where(merged.astype(jnp.float32) > 0, cotangent, 0.0).astype(jnp.bfloat16)
    grad_out_ref[...] = grad_out
    back = dot_f32(grad_out, merge_ref[...], 1, 1)
    kept = jnp.where(joined.astype(jnp.float32) > 0, back, 0.0).astype(jnp.bfloat16)
    dilated = kept[:, branch:]
    dilated_ref[...] = dilated
    gradient_ref[:, :branch] = kept[:, :branch]
    for j in range(3):
        moved = moved_rows(dilated.astype(jnp.float32), width, (1 - j) * DILATION_RATE)
        gradient_ref[:, (1 + j) * branch : (2 + j) * branch] = moved.astype(jnp.bfloat16)


def head(width, centre, above, below, bias, whole_merge, merge_bias, cotangent):
    pixels, branch = above.shape
    merged_width = whole_merge.shape[1]
    widths = (merged_width, branch, 4 * branch, 2 * branch, merged_width)
    operands = (centre, above, below, bias, whole_merge, merge_bias.reshape(1, -1), cotangent)
    return pl.pallas_call(
        functools.partial(head_kernel, width),
        out_shape=[jax.ShapeDtypeStruct((pixels, w), jnp.bfloat16) for w in widths],
        in_specs=[pl.BlockSpec(memory_space=pltpu.VMEM)] * len(operands),
        out_specs=[pl.BlockSpec(memory_space=pltpu.VMEM)] * len(widths),
        cost_estimate=pl.CostEstimate(
            flops=8 * pixels * branch * merged_width,
            bytes_accessed=8 * pixels * (6 * branch + merged_width),
            transcendentals=0,
        ),
        compiler_params=pltpu.CompilerParams(vmem_limit_bytes=12 << 20),
        name="head",
    )(*operands)


def is_upward(me, step):
    return me // step % 2 == 0


def column_sum(ref, width, branch):
    total = None
    for j in range(3):
        moved = moved_rows(ref[:, j * branch : (j + 1) * branch], width, (j - 1) * DILATION_RATE)
        total = moved if total is None else total + moved
    return total


def partner_kernel(width, first_ref, second_ref, out_ref):
    pixels, branch = first_ref.shape[0], out_ref.shape[1]
    out_ref[0:pixels, :] = column_sum(first_ref, width, branch)
    out_ref[pixels : 2 * pixels, :] = column_sum(second_ref, width, branch)


def partner_sums(width, products):
    pixels, lanes = products[0].shape
    out = [jax.ShapeDtypeStruct((2 * pixels, lanes // 3), jnp.float32)]
    kernel = functools.partial(partner_kernel, width)
    return local_call(kernel, "partner_sums", out, products, 16 * pixels * lanes, 8)[0]


def halo_kernel(width, step, me_ref, first_ref, second_ref, came_ref, first_out_ref, second_out_ref):
    pixels, branch = first_out_ref.shape
    sums = [
        column_sum(ref, width, branch) + came_ref[k * pixels : (k + 1) * pixels, :]
        for k, ref in enumerate((first_ref, second_ref))
    ]
    upward = is_upward(me_ref[0], step)
    first_out_ref[...] = jnp.where(upward, sums[0], sums[1])
    second_out_ref[...] = jnp.where(upward, sums[1], sums[0])


def halo_sums(width, step, products, came, me):
    pixels, taps = products[0].shape
    out = jax.ShapeDtypeStruct((pixels, taps // 3), jnp.float32)
    kernel = functools.partial(halo_kernel, width, step)
    return halo_call(kernel, "halo_sums", out, me, *products, came)


def shift_kernel(width, step, flip, me_ref, first_ref, second_ref, first_out_ref, second_out_ref):
    branch = first_ref.shape[1]
    upward = is_upward(me_ref[0] ^ flip, step)
    first, second = first_ref[...].astype(jnp.float32), second_ref[...].astype(jnp.float32)
    pairs = ((first, second, first_out_ref), (second, first, second_out_ref))
    for here, there, out_ref in pairs:
        block = jnp.where(upward, here, there)
        for j in range(3):
            moved = moved_rows(block, width, (1 - j) * DILATION_RATE)
            out_ref[:, j * branch : (j + 1) * branch] = moved.astype(jnp.bfloat16)


def shifted(width, step, first, second, me, flip=0):
    pixels, branch = first.shape
    out = jax.ShapeDtypeStruct((pixels, 3 * branch), jnp.bfloat16)
    kernel = functools.partial(shift_kernel, width, step, flip)
    return halo_call(kernel, "shift", out, me, first, second)


def halo_call(kernel, name, out, me, first, *others):
    return pl.pallas_call(
        kernel,
        out_shape=(out, out),
        in_specs=[pl.BlockSpec(memory_space=pltpu.SMEM)]
        + [pl.BlockSpec(memory_space=pltpu.VMEM)] * (1 + len(others)),
        out_specs=(pl.BlockSpec(memory_space=pltpu.VMEM),) * 2,
        cost_estimate=pl.CostEstimate(
            flops=0, bytes_accessed=8 * (first.size + out.size), transcendentals=0
        ),
        compiler_params=pltpu.CompilerParams(vmem_limit_bytes=8 << 20),
        name=name,
    )(me.reshape(1), first, *others)


def merge_gradient_kernel(me_ref, joined_ref, grad_out_ref, own_ref, other_ref, total_ref):
    me = me_ref[0]
    total_ref[...] = dot_f32(joined_ref[...], grad_out_ref[...], 0, 0)
    half = own_ref.shape[0]
    group = 8
    for k in range(half // group):
        here = slice(k * group, (k + 1) * group)
        device = (2 * k) ^ me
        own_ref[here, :] = total_ref[pl.ds(pl.multiple_of(device * group, group), group), :]
        device = (2 * k + 1) ^ me
        other_ref[here, :] = total_ref[pl.ds(pl.multiple_of(device * group, group), group), :]


def merge_gradient(joined, grad_out, me):
    pixels, width = joined.shape
    half = jax.ShapeDtypeStruct((width // 2, grad_out.shape[1]), jnp.float32)
    return pl.pallas_call(
        merge_gradient_kernel,
        out_shape=(half, half),
        in_specs=[pl.BlockSpec(memory_space=pltpu.SMEM)]
        + [pl.BlockSpec(memory_space=pltpu.VMEM)] * 2,
        out_specs=(pl.BlockSpec(memory_space=pltpu.VMEM),) * 2,
        scratch_shapes=[pltpu.VMEM((width, grad_out.shape[1]), jnp.float32)],
        cost_estimate=pl.CostEstimate(
            flops=2 * pixels * width * grad_out.shape[1],
            bytes_accessed=8 * pixels * width,
            transcendentals=0,
        ),
        compiler_params=pltpu.CompilerParams(vmem_limit_bytes=8 << 20),
        name="merge_gradient",
    )(me.reshape(1), joined, grad_out)


def layout(rows, merge_rows, merge_width):
    shares = (0, rows // 4, 3 * rows // 8, rows)
    tables = []
    for p, portion in enumerate(PORTIONS):
        table = [(k, 0, n * rows, rows) for n, k in enumerate(k for k in portion if k > 0)]
        table.append((0, shares[p], 3 * rows, shares[p + 1] - shares[p]))
        if p == 2:
            first = 3 * rows + table[-1][3]
            lanes = range(0, merge_width, LANES)
            table += [(None, x, first + n * merge_rows, merge_rows) for n, x in enumerate(lanes)]
        tables.append(table)
    return tables


def stack_rows(table):
    return table[-1][2] + table[-1][3]


def lanes_of(k):
    for p, portion in enumerate(PORTIONS):
        if k in portion:
            at = portion.index(k) * LANES
            return p, slice(at, at + LANES)


def local_call(kernel, name, out_shape, operands, moved, grant):
    return pl.pallas_call(
        kernel,
        out_shape=out_shape,
        in_specs=[pl.BlockSpec(memory_space=pltpu.VMEM)] * len(operands),
        out_specs=[pl.BlockSpec(memory_space=pltpu.VMEM)] * len(out_shape),
        cost_estimate=pl.CostEstimate(flops=moved // 4, bytes_accessed=moved, transcendentals=0),
        compiler_params=pltpu.CompilerParams(vmem_limit_bytes=grant << 20),
        name=name,
    )(*operands)


def pack_kernel(tables, weight_ref, merge_ref, out_ref, sems):
    copies, base = [], 0
    for table in tables:
        for k, there, here, count in table:
            if k is None:
                source = merge_ref.at[:, pl.ds(there, LANES)]
            else:
                source = weight_ref.at[k, pl.ds(there, count), :]
            target = out_ref.at[pl.ds(base + here, count), :]
            copies.append(pltpu.make_async_copy(source, target, sems.at[len(copies)]))
        base += stack_rows(table)
    for copy in copies:
        copy.start()
    for copy in copies:
        copy.wait()


def pack(weight, merge_weight, tables):
    return pl.pallas_call(
        functools.partial(pack_kernel, tables),
        out_shape=jax.ShapeDtypeStruct((sum(map(stack_rows, tables)), LANES), weight.dtype),
        in_specs=[pl.BlockSpec(memory_space=pltpu.HBM)] * 2,
        out_specs=pl.BlockSpec(memory_space=pltpu.VMEM),
        scratch_shapes=[pltpu.SemaphoreType.DMA((sum(map(len, tables)),))],
        cost_estimate=pl.CostEstimate(flops=0, bytes_accessed=4 * weight.size, transcendentals=0),
        compiler_params=pltpu.CompilerParams(vmem_limit_bytes=4 << 20),
        name="pack",
    )(*(pltpu.with_memory_space_constraint(x, pltpu.HBM) for x in (weight, merge_weight)))


def block_pair(target, inner):
    low = target // inner * (2 * inner) + target % inner
    return low, low + inner


def unpack_kernel(tables, inners, *refs):
    outs = refs[6:]

    def step(target, carry):
        for p, table in enumerate(tables):
            for ref, block in zip(refs[2 * p : 2 * p + 2], block_pair(target, inners[p])):
                for k, there, here, count in table:
                    value = ref[target, here : here + count, :]
                    if k is None:
                        outs[3][block, :, there : there + LANES] = value
                    else:
                        q, lanes = lanes_of(k)
                        outs[q][block, there : there + count, lanes] = value
        return carry

    lax.fori_loop(0, refs[0].shape[0], step, 0)


def unpack(pairs, tables, inners, rows, merge_rows, merge_width):
    blocks = 2 * pairs[0].shape[0]
    shapes = [(blocks, rows, LANES * len(p)) for p in PORTIONS] + [(blocks, merge_rows, merge_width)]
    out = [jax.ShapeDtypeStruct(x, jnp.bfloat16) for x in shapes]
    kernel = functools.partial(unpack_kernel, tables, tuple(inners))
    return local_call(kernel, "unpack", out, pairs, 4 * sum(x.size for x in pairs), 16)


def first_fold_kernel(tables, inners, *refs):
    owns, arrived, keeps, sends = refs[:4], refs[4], refs[5:8], refs[8:]

    def step(target, carry):
        for p, table in enumerate(tables):
            for half, block in enumerate(block_pair(target, inners[p])):
                for k, there, here, count in table:
                    if k is None:
                        q, at = 3, (block, slice(None), slice(there, there + LANES))
                    else:
                        q, lanes = lanes_of(k)
                        at = (block, slice(there, there + count), lanes)
                    value = owns[q][at]
                    if k is None:
                        value = value + arrived[at]
                    out_ref = (keeps, sends)[half][p]
                    out_ref[target, here : here + count, :] = value.astype(out_ref.dtype)
        return carry

    lax.fori_loop(0, keeps[0].shape[0], step, 0)


def fold_kernel(inners, *refs):
    owns, arriveds, keeps, sends = (refs[3 * k : 3 * k + 3] for k in range(4))

    def step(target, carry):
        for p in range(3):
            for half, block in enumerate(block_pair(target, inners[p])):
                value = owns[p][block] + arriveds[p][block].astype(jnp.float32)
                out_ref = (keeps, sends)[half][p]
                out_ref[target] = value.astype(out_ref.dtype)
        return carry

    lax.fori_loop(0, keeps[0].shape[0], step, 0)


def fold(owns, arriveds, tables, inners):
    shapes = [(owns[0].shape[0] // 2, stack_rows(table), LANES) for table in tables]
    out = [jax.ShapeDtypeStruct(x, t) for t in (jnp.float32, jnp.bfloat16) for x in shapes]
    if len(owns) == 4:
        kernel = functools.partial(first_fold_kernel, tables, tuple(inners))
    else:
        kernel = functools.partial(fold_kernel, tuple(inners))
    moved = 9 * sum(x.size for x in owns)
    out = local_call(kernel, "fold", out, (*owns, *arriveds), moved, 20)
    return out[:3], out[3:]


def last_fold_kernel(*refs):
    owns, arriveds = refs[:3], refs[3:6]
    base = 0
    for own, arrived in zip(owns, arriveds):
        at = slice(base, base + own.shape[1])
        base += own.shape[1]
        refs[6][at, :] = own[0] + arrived[0].astype(jnp.float32)
        refs[7][at, :] = (own[1] + arrived[1].astype(jnp.float32)).astype(jnp.bfloat16)


def last_fold(owns, arriveds):
    shape = (sum(x.shape[1] for x in owns), LANES)
    out = [jax.ShapeDtypeStruct(shape, t) for t in (jnp.float32, jnp.bfloat16)]
    moved = 9 * sum(x.size for x in owns)
    return local_call(last_fold_kernel, "last_fold", out, (*owns, *arriveds), moved, 8)


def scaled_kernel(tables, scale, keep_ref, arrived_ref, out_ref, out_merge_ref):
    base = 0
    for table in tables:
        for k, there, here, count in table:
            at = slice(base + here, base + here + count)
            value = (keep_ref[at, :] + arrived_ref[at, :].astype(jnp.float32)) * scale
            if k is None:
                out_merge_ref[:, there : there + LANES] = value
            else:
                out_ref[k, there : there + count, :] = value
        base += stack_rows(table)


def scaled(keep, arrived, tables, scale, rows, merge_rows, merge_width):
    taps = sum(map(len, PORTIONS))
    out = [
        jax.ShapeDtypeStruct((taps, rows, LANES), jnp.float32),
        jax.ShapeDtypeStruct((merge_rows, merge_width), jnp.float32),
    ]
    kernel = functools.partial(scaled_kernel, tables, scale)
    return local_call(kernel, "scaled", out, (keep, arrived), 10 * keep.size, 8)


def column_shifted(rows, shift):
    width = rows.shape[1]
    if shift == 0:
        return rows
    if shift > 0:
        return jnp.pad(rows[:, shift:], ((0, 0), (0, shift), (0, 0)))
    return jnp.pad(rows[:, : width + shift], ((0, 0), (-shift, 0), (0, 0)))


def on_device(
    features, branch_kernel_weight, branch_norm_bias, merge_weight, merge_bias, cotangent
):
    device_count = lax.axis_size("row")
    bit_count = device_count.bit_length() - 1
    me = lax.axis_index("row")
    rows, width, channels = features.shape
    taps, branch = branch_kernel_weight.shape[1:]
    own_channels = branch_kernel_weight.shape[0]
    joined_rows, merged_width = merge_weight.shape
    joined_width = joined_rows * device_count
    pixels = rows * width
    scale = 1.0 / math.sqrt(rows * device_count * width)
    device_step = DILATION_RATE // rows
    bits = (1,) * (bit_count - 1)
    orders = bit_orders(bit_count)
    far_bits = list(range(bit_count - 1, 3, -1))
    paired = 2 * own_channels == LANES and joined_rows == 8 and branch == LANES and bit_count == 5
    portion_widths = [len(p) * branch for p in PORTIONS]

    def split(array, widths):
        starts = [sum(widths[:i]) for i in range(len(widths))]
        return [lax.slice_in_dim(array, s, s + w, axis=-1) for s, w in zip(starts, widths)]

    tap_order = [k for portion in PORTIONS for k in portion]
    weight = branch_kernel_weight.transpose(1, 0, 2)
    half_rows = channels // 2
    crossing = orders + [orders[1]]
    flat = features.reshape(pixels, channels)
    if paired:
        tables = layout(own_channels, joined_rows, merged_width)
        block = pack(weight, merge_weight, tables)
        block, flat, me = together(block, flat, me)
        flat_own, flat_other = reordered(flat, me)
        block = block.reshape(bits + block.shape)
        (arrived,) = together(exchanged(block, far_bits[0]))
        block, arrived, flat_own, flat_other = together(block, arrived, flat_own, flat_other)
        blocks, base = [], 0
        for table in tables:
            parts = [
                lax.slice_in_dim(x, base, base + stack_rows(table), axis=-2) for x in (block, arrived)
            ]
            blocks.append(jnp.concatenate(parts, axis=0))
            base += stack_rows(table)
        for step in range(len(orders[0]) - 1):
            blocks = gathered(together(*blocks), [o[step] for o in orders], bit_count)
        *blocks, flat_partner = together(*blocks, exchanged(flat_other, 0))
        arrived = together(*[exchanged(b, o[-1]) for b, o in zip(blocks, orders)])
        pairs = [
            x.reshape((device_count // 4,) + x.shape[-2:])
            for pair in zip(blocks, arrived)
            for x in pair
        ]
        inners = [1 << (o[-1] - 1) for o in orders]
        *own_weight, own_merge = unpack(
            pairs, tables, inners, own_channels, joined_rows, merged_width
        )
        own_weight = [x.reshape(half_rows, x.shape[-1]) for x in own_weight]
    else:
        block = jnp.concatenate([weight[k] for k in tap_order], axis=1)
        to_relative = relative_order(channels, device_count, me)
        flat = dot_f32(flat, to_relative, 1, 0).astype(jnp.bfloat16)
        flat_own, flat_other = flat[:, :half_rows], flat[:, half_rows:]
        block = block.reshape(bits + block.shape)
        merge_block = merge_weight.reshape(bits + merge_weight.shape)
        for bit in far_bits:
            block, merge_block = gathered([block, merge_block], [bit, bit], bit_count)
        blocks = split(block, portion_widths) + [merge_block]
        for step in range(len(orders[0])):
            blocks = gathered(together(*blocks), [o[step] for o in crossing], bit_count)
        own_merge = blocks.pop()
        own_weight = [b.reshape(half_rows, b.shape[-1]) for b in blocks]
    own_merge = own_merge.reshape(joined_width // 2, merged_width)

    def row_sum(parts):
        total = None
        for j, part in enumerate(parts):
            moved = column_shifted(part.reshape(rows, width, branch), (j - 1) * DILATION_RATE)
            total = moved if total is None else total + moved
        return total

    def by_tap(product):
        return split(product, [branch] * (product.shape[1] // branch))

    upward = is_upward(me, device_step)
    if paired:
        sums = partner_sums(width, [dot_f32(flat_partner, w, 1, 0) for w in own_weight[:2]])
        sums, own_weight[0], own_weight[1] = together(sums, *own_weight[:2])
        products = [dot_f32(flat_own, w, 1, 0) for w in own_weight[:2]]
        came, *products = together(exchanged(sums, 0), *products)
        sums = halo_sums(width, device_step, products, came, me)
        other_weight = [None, None]
    else:
        other_weight = [exchanged(w, 0) for w in own_weight[:2]]
        sums = [
            dot_f32(flat_own, a, 1, 0) + dot_f32(flat_other, b, 1, 0)
            for a, b in zip(own_weight, other_weight)
        ]
        sums = [row_sum(by_tap(x)).reshape(pixels, branch) for x in sums]
        sums = [jnp.where(upward, *sums), jnp.where(upward, *sums[::-1])]
    merge_to_relative = relative_order(joined_width, device_count, me)
    own_weight[2], own_merge, *sums = together(own_weight[2], own_merge, *sums)
    whole_merge = dot_f32(
        merge_to_relative, jnp.concatenate([own_merge, exchanged(own_merge, 0)], axis=0), 1, 0
    ).astype(jnp.bfloat16)
    other_weight.append(exchanged(own_weight[2], 0))
    centre = dot_f32(flat_own, own_weight[2], 1, 0) + dot_f32(flat_other, other_weight[2], 1, 0)
    above, below = swapped(sums[0], device_step, 0), swapped(sums[1], device_step, 1)
    flat_cotangent = cotangent.reshape(pixels, merged_width)
    if paired:
        merged, grad_dil, centre_gradient, joined, grad_out = head(
            width, centre, above, below, branch_norm_bias, whole_merge, merge_bias, flat_cotangent
        )
    else:
        centre = by_tap(centre)
        z_dil = row_sum(centre[1:]).reshape(pixels, branch) + above + below
        act_one = jnp.maximum(centre[0] + branch_norm_bias[0], 0.0).astype(jnp.bfloat16)
        act_dil = jnp.maximum(z_dil + branch_norm_bias[1], 0.0).astype(jnp.bfloat16)
        joined = jnp.concatenate([act_one, act_dil], axis=1)
        merged = jnp.maximum(dot_f32(joined, whole_merge, 1, 0) + merge_bias, 0.0)
        merged = merged.astype(jnp.bfloat16)
        grad_out = jnp.where(merged > 0, flat_cotangent, jnp.zeros((), jnp.bfloat16))
        back = dot_f32(grad_out, whole_merge, 1, 1)
        kept = jnp.where(joined > 0, back, 0.0).astype(jnp.bfloat16)
        grad_dil = kept[:, branch:]
        centre_gradient = None

    def shifted_gradients(block):
        block = block.reshape(rows, width, branch)
        parts = [column_shifted(block, (1 - j) * DILATION_RATE) for j in range(3)]
        return [part.reshape(pixels, branch) for part in parts]

    if not paired:
        centre_gradient = jnp.concatenate([kept[:, :branch]] + shifted_gradients(grad_dil), axis=1)
    halos = [swapped(grad_dil, device_step, 0), swapped(grad_dil, device_step, 1)]
    if paired:
        own_merge, other_merge = merge_gradient(joined, grad_out, me)
    else:
        joined_relative = dot_f32(joined, merge_to_relative, 1, 0).astype(jnp.bfloat16)
        merge_total = dot_f32(joined_relative, grad_out, 0, 0)
        own_merge = merge_total[: joined_width // 2]
        other_merge = merge_total[joined_width // 2 :]
    merge_arrived = exchanged(other_merge, 0)

    centre_gradient, own_merge = together(centre_gradient, own_merge)
    own_total, other_total = [None] * 3, [None] * 3
    own_total[2] = dot_f32(flat_own, centre_gradient, 0, 0)
    if paired:
        partner_gradient = exchanged(centre_gradient, 0)
        own_total[2] = own_total[2] + dot_f32(flat_partner, partner_gradient, 0, 0)
        other_weight[:2] = [exchanged(w, 0) for w in own_weight[:2]]
        *halos, own_total[2], other_weight[0], other_weight[1] = together(
            *halos, own_total[2], *other_weight[:2]
        )
        partner_halos = [exchanged(h, 0) for h in halos]
        gradients = [*shifted(width, device_step, *halos, me), centre_gradient]
        own_total[:2] = [dot_f32(flat_own, g, 0, 0) for g in gradients[:2]]
        *partner_halos, own_total[0], own_total[1] = together(*partner_halos, *own_total[:2])
        partner_gradients = shifted(width, device_step, *partner_halos, me, 1)
        for p in range(2):
            own_total[p] = own_total[p] + dot_f32(flat_partner, partner_gradients[p], 0, 0)
    else:
        other_total[2] = dot_f32(flat_other, centre_gradient, 0, 0).astype(jnp.bfloat16)
        *halos, own_total[2], other_total[2] = together(*halos, own_total[2], other_total[2])
        halos = [jnp.where(upward, *halos), jnp.where(upward, *halos[::-1])]
        gradients = [jnp.concatenate(shifted_gradients(h), axis=1) for h in halos]
        gradients = together(*gradients) + [centre_gradient]
        for p in range(2):
            other_total[p] = dot_f32(flat_other, gradients[p], 0, 0).astype(jnp.bfloat16)
            own_total[p] = dot_f32(flat_own, gradients[p], 0, 0)
    if paired:
        own_blocks = device_count // 2
        owns = [x.reshape(own_blocks, -1, x.shape[-1]) for x in (*own_total, own_merge)]
        arrived = [merge_arrived.reshape(owns[3].shape)]
        left = [list(range(bit_count - 1, 0, -1)) for _ in orders]
        for step in range(len(orders[0])):
            bits_now = [o[-1 - step] for o in orders]
            inners = [1 << (len(x) - 1 - x.index(b)) for x, b in zip(left, bits_now)]
            owns, sent = fold(owns, arrived, tables, inners)
            for x, b in zip(left, bits_now):
                x.remove(b)
            if step == 0:
                *sent, g0, g1, g2 = together(*sent, *gradients)
                input_grad = input_gradient([g0, g1, g2], own_weight, other_weight, me)
            else:
                sent = together(*sent)
            arrived = together(*[exchanged(t, b) for t, b in zip(sent, bits_now)])
            if step == 0:
                *arrived, input_grad = together(*arrived, input_grad)
        keep, sent = last_fold(owns, arrived)
        branch_kernel_gradient, grad_merge = scaled(
            keep,
            exchanged(sent, far_bits[0]),
            tables,
            scale,
            own_channels,
            joined_rows,
            merged_width,
        )
        branch_kernel_gradient = branch_kernel_gradient.transpose(1, 0, 2)
    else:
        merge_total = own_merge + merge_arrived.astype(jnp.float32)
        merge_total = merge_total.reshape((2,) * (bit_count - 1) + (joined_rows, merged_width))
        merge_parts = halves(merge_total, far_bits[0], bit_count) if far_bits else None
        sending = list(other_total) + ([merge_parts[1]] if far_bits else [])
        arrived = [
            exchanged(t, b) for t, b in zip(together(*sending), [0, 0, 0] + far_bits[:1])
        ]
        arrived = together(*arrived)
        if far_bits:
            merge_total = merge_parts[0] + arrived.pop().astype(jnp.float32)
        for bit in far_bits[1:]:
            own, other = halves(merge_total, bit, bit_count)
            merge_total = own + exchanged(other, bit).astype(jnp.float32)
        totals = []
        for own, a, o in zip(own_total, arrived, orders):
            shape = (2,) * (bit_count - 1) + (own.shape[0] // (device_count // 2), own.shape[1])
            totals.append(added(own.reshape(shape), a.reshape(shape), o[-1], bit_count))
        totals.append(halves(merge_total, crossing[3][-1], bit_count))
        *sent, g0, g1, g2 = together(*[t[1] for t in totals], *gradients)
        input_total = sum(
            dot_f32(g, jnp.concatenate([a, b], axis=0), 1, 1)
            for g, a, b in zip((g0, g1, g2), own_weight, other_weight)
        ).astype(jnp.bfloat16)
        input_grad = dot_f32(input_total, to_relative, 1, 1).astype(jnp.bfloat16)
        for step in range(len(orders[0])):
            arrived = together(*[exchanged(t, o[-1 - step]) for t, o in zip(sent, crossing)])
            if step == 0:
                *arrived, input_grad = together(*arrived, input_grad)
            own = [t[0] for t in totals]
            if step + 1 < len(orders[0]):
                totals = [
                    added(t, a, o[-2 - step], bit_count) for t, a, o in zip(own, arrived, crossing)
                ]
                sent = together(*[t[1] for t in totals])
            else:
                totals = [t + a.astype(jnp.float32) for t, a in zip(own, arrived)]
        grad_merge = totals[3].reshape(joined_rows, merged_width) * scale
        total = jnp.concatenate(totals[:3], axis=-1)
        for bit in far_bits[::-1]:
            own, other = halves(total, bit, bit_count)
            total = own + exchanged(other, bit).astype(jnp.float32)
        weight_gradient = dict(
            zip([k for p in PORTIONS for k in p], by_tap(total.reshape(own_channels, -1)))
        )
        branch_kernel_gradient = jnp.stack([weight_gradient[k] for k in range(taps)], axis=1) * scale

    return (
        merged.reshape(rows, width, merged_width),
        input_grad.reshape(rows, width, channels),
        branch_kernel_gradient,
        grad_merge,
    )


def solution(mesh):
    placed = (
        P(("grp", "row"), None, None),
        P("row", None, None),
        P(),
        P("row", None),
        P(),
        P(("grp", "row"), None, None),
    )
    return jax.shard_map(
        on_device,
        mesh=mesh,
        in_specs=placed,
        out_specs=(
            P(("grp", "row"), None, None),
            P(("grp", "row"), None, None),
            P(("grp", "row"), None, None),
            P(("grp", "row"), None),
        ),
        check_vma=False,
    )
```

```python
import functools
import math

import jax
import jax.numpy as jnp
from jax import lax
from jax.experimental import pallas as pl
from jax.experimental.pallas import tpu as pltpu
from jax.sharding import PartitionSpec as P

DILATION_RATE = 18
LANES = 128
PORTIONS = ((1, 2, 3), (7, 8, 9), (0, 4, 5, 6))


def swapped(block, distance, parity):
    count = lax.axis_size("row")
    pairs = [(i, i + distance) for i in range(count - distance) if i // distance % 2 == parity]
    return lax.ppermute(block, "row", pairs + [(b, a) for a, b in pairs])


def exchanged(block, bit):
    return lax.ppermute(block, "row", [(i, i ^ (1 << bit)) for i in range(lax.axis_size("row"))])


def dot_f32(left, right, left_dim, right_dim):
    return lax.dot_general(
        left, right, (((left_dim,), (right_dim,)), ((), ())), preferred_element_type=jnp.float32
    )


def bit_orders(bit_count):
    near = [b for b in (3, 2, 1) if b < bit_count]
    return [near[k:] + near[:k] for k in range(3)]


def axis_of(bit, bit_count):
    return bit_count - 1 - bit


def after(value, *others):
    return lax.optimization_barrier((value,) + others)[0]


def together(*values):
    return list(lax.optimization_barrier(values))


def gathered(blocks, crossed, bit_count):
    arrived = together(*[exchanged(b, bit) for b, bit in zip(blocks, crossed)])
    return [
        jnp.concatenate([b, a], axis=axis_of(bit, bit_count))
        for b, a, bit in zip(blocks, arrived, crossed)
    ]


def added(own, arrived, bit, bit_count):
    axis = axis_of(bit, bit_count)

    def half(k):
        parts = [lax.slice_in_dim(x, k, k + 1, axis=axis) for x in (own, arrived)]
        return parts[0] + parts[1].astype(jnp.float32)

    return half(0), half(1).astype(jnp.bfloat16)


def halves(block, bit, bit_count):
    axis = axis_of(bit, bit_count)
    return (
        lax.slice_in_dim(block, 0, 1, axis=axis),
        lax.slice_in_dim(block, 1, 2, axis=axis).astype(jnp.bfloat16),
    )


def relative_order(size, device_count, me):
    width = size // device_count
    target = lax.broadcasted_iota(jnp.int32, (size, size), 1)
    source = lax.broadcasted_iota(jnp.int32, (size, size), 0)
    half = device_count // 2
    block, inner = target // width, target % width
    device = (block % half) * 2 + block // half
    return (source == (device ^ me) * width + inner).astype(jnp.bfloat16)


def reorder_kernel(me_ref, x_ref, own_ref, other_ref):
    me = me_ref[0]
    chip, core = me // 2, me % 2
    lane = lax.broadcasted_iota(jnp.int32, (x_ref.shape[0], LANES), 1)
    low_lane = lane < LANES // 2

    def tile(block):
        start = pl.multiple_of((block ^ chip) * LANES, LANES)
        return x_ref[:, pl.ds(start, LANES)].astype(jnp.float32)

    for t in range(own_ref.shape[1] // LANES):
        first, second = tile(2 * t), tile(2 * t + 1)
        low = jnp.where(low_lane, first, pltpu.roll(second, LANES // 2, 1)).astype(jnp.bfloat16)
        high = jnp.where(low_lane, pltpu.roll(first, LANES // 2, 1), second).astype(jnp.bfloat16)
        columns = slice(t * LANES, (t + 1) * LANES)
        own_ref[:, columns] = jnp.where(core == 0, low, high)
        other_ref[:, columns] = jnp.where(core == 0, high, low)


def reordered(flat, me):
    pixels, channels = flat.shape
    half = jax.ShapeDtypeStruct((pixels, channels // 2), flat.dtype)
    return pl.pallas_call(
        reorder_kernel,
        out_shape=(half, half),
        in_specs=[
            pl.BlockSpec(memory_space=pltpu.SMEM),
            pl.BlockSpec(memory_space=pltpu.VMEM),
        ],
        out_specs=(pl.BlockSpec(memory_space=pltpu.VMEM),) * 2,
        cost_estimate=pl.CostEstimate(
            flops=8 * pixels * channels, bytes_accessed=4 * pixels * channels, transcendentals=0
        ),
        compiler_params=pltpu.CompilerParams(vmem_limit_bytes=12 << 20),
        name="reorder",
    )(me.reshape(1), flat)


def input_gradient_kernel(portion_count, me_ref, *refs):
    me = me_ref[0]
    chip, core = me // 2, me % 2
    gradients = refs[:portion_count]
    own, other = refs[portion_count : 2 * portion_count], refs[2 * portion_count : -3]
    merged_ref, out_ref, merged_out_ref = refs[-3:]
    merged_out_ref[...] = merged_ref[...]
    rows = LANES // 2

    def step(t, carry):
        total = None
        for p in range(portion_count):
            taken = []
            for k in range(2):
                at = pl.ds(pl.multiple_of(((2 * t + k) ^ chip) * rows, rows), rows)
                a, b = own[p][at, :], other[p][at, :]
                taken += [jnp.where(core == 0, a, b), jnp.where(core == 0, b, a)]
            part = dot_f32(gradients[p][...], jnp.concatenate(taken, axis=0), 1, 1)
            total = part if total is None else total + part
        columns = pl.ds(pl.multiple_of(t * 2 * LANES, 2 * LANES), 2 * LANES)
        out_ref[:, columns] = total.astype(out_ref.dtype)
        return carry

    lax.fori_loop(0, out_ref.shape[1] // (2 * LANES), step, 0, unroll=True)


def input_gradient(gradients, own, other, me, merged):
    pixels = gradients[0].shape[0]
    half = own[0].shape[0]
    operands = [pltpu.with_memory_space_constraint(x, pltpu.VMEM) for x in (*gradients, *own, *other, merged)]
    columns = sum(g.shape[1] for g in gradients)
    return pl.pallas_call(
        functools.partial(input_gradient_kernel, len(gradients)),
        out_shape=(
            jax.ShapeDtypeStruct((pixels, 2 * half), jnp.bfloat16),
            jax.ShapeDtypeStruct(merged.shape, merged.dtype),
        ),
        in_specs=[pl.BlockSpec(memory_space=pltpu.SMEM)]
        + [pl.BlockSpec(memory_space=pltpu.VMEM)] * len(operands),
        out_specs=(pl.BlockSpec(memory_space=pltpu.VMEM),) * 2,
        cost_estimate=pl.CostEstimate(
            flops=4 * pixels * columns * half,
            bytes_accessed=2 * (pixels * columns + 2 * half * columns + 2 * pixels * half),
            transcendentals=0,
        ),
        compiler_params=pltpu.CompilerParams(vmem_limit_bytes=16 << 20),
        name="input_gradient",
    )(me.reshape(1), *operands)


def moved_rows(block, width, shift):
    if shift == 0:
        return block
    size = block.shape[0]
    column = lax.broadcasted_iota(jnp.int32, block.shape, 0) % width + shift
    inside = (column >= 0) & (column < width)
    return jnp.where(inside, pltpu.roll(block, (-shift) % size, 0), 0.0)


def head_kernel(
    width, centre_ref, above_ref, below_ref, bias_ref, merge_ref, merge_bias_ref, cotangent_ref,
    merged_ref, dilated_ref, gradient_ref, joined_ref, grad_out_ref,
):
    branch = above_ref.shape[1]
    z_dil = above_ref[...] + below_ref[...]
    for j in range(3):
        part = centre_ref[:, (1 + j) * branch : (2 + j) * branch]
        z_dil = z_dil + moved_rows(part, width, (j - 1) * DILATION_RATE)
    act_one = jnp.maximum(centre_ref[:, :branch] + bias_ref[0:1, :], 0.0).astype(jnp.bfloat16)
    act_dil = jnp.maximum(z_dil + bias_ref[1:2, :], 0.0).astype(jnp.bfloat16)
    joined = jnp.concatenate([act_one, act_dil], axis=1)
    joined_ref[...] = joined
    merged = jnp.maximum(dot_f32(joined, merge_ref[...], 1, 0) + merge_bias_ref[...], 0.0)
    merged = merged.astype(jnp.bfloat16)
    merged_ref[...] = merged
    cotangent = cotangent_ref[...].astype(jnp.float32)
    grad_out = jnp.where(merged.astype(jnp.float32) > 0, cotangent, 0.0).astype(jnp.bfloat16)
    grad_out_ref[...] = grad_out
    back = dot_f32(grad_out, merge_ref[...], 1, 1)
    kept = jnp.where(joined.astype(jnp.float32) > 0, back, 0.0).astype(jnp.bfloat16)
    dilated = kept[:, branch:]
    dilated_ref[...] = dilated
    gradient_ref[:, :branch] = kept[:, :branch]
    for j in range(3):
        moved = moved_rows(dilated.astype(jnp.float32), width, (1 - j) * DILATION_RATE)
        gradient_ref[:, (1 + j) * branch : (2 + j) * branch] = moved.astype(jnp.bfloat16)


def head(width, centre, above, below, bias, whole_merge, merge_bias, cotangent):
    pixels, branch = above.shape
    merged_width = whole_merge.shape[1]
    widths = (merged_width, branch, 4 * branch, 2 * branch, merged_width)
    operands = (centre, above, below, bias, whole_merge, merge_bias.reshape(1, -1), cotangent)
    return pl.pallas_call(
        functools.partial(head_kernel, width),
        out_shape=[jax.ShapeDtypeStruct((pixels, w), jnp.bfloat16) for w in widths],
        in_specs=[pl.BlockSpec(memory_space=pltpu.VMEM)] * len(operands),
        out_specs=[pl.BlockSpec(memory_space=pltpu.VMEM)] * len(widths),
        cost_estimate=pl.CostEstimate(
            flops=8 * pixels * branch * merged_width,
            bytes_accessed=8 * pixels * (6 * branch + merged_width),
            transcendentals=0,
        ),
        compiler_params=pltpu.CompilerParams(vmem_limit_bytes=12 << 20),
        name="head",
    )(*operands)


def is_upward(me, step):
    return me // step % 2 == 0


def column_sum(ref, width, branch):
    total = None
    for j in range(3):
        moved = moved_rows(ref[:, j * branch : (j + 1) * branch], width, (j - 1) * DILATION_RATE)
        total = moved if total is None else total + moved
    return total


def partner_kernel(width, first_ref, second_ref, out_ref):
    pixels, branch = first_ref.shape[0], out_ref.shape[1]
    out_ref[0:pixels, :] = column_sum(first_ref, width, branch)
    out_ref[pixels : 2 * pixels, :] = column_sum(second_ref, width, branch)


def partner_sums(width, products):
    pixels, lanes = products[0].shape
    out = [jax.ShapeDtypeStruct((2 * pixels, lanes // 3), jnp.float32)]
    kernel = functools.partial(partner_kernel, width)
    return local_call(kernel, "partner_sums", out, products, 16 * pixels * lanes, 8)[0]


def halo_kernel(width, step, me_ref, first_ref, second_ref, came_ref, first_out_ref, second_out_ref):
    pixels, branch = first_out_ref.shape
    sums = [
        column_sum(ref, width, branch) + came_ref[k * pixels : (k + 1) * pixels, :]
        for k, ref in enumerate((first_ref, second_ref))
    ]
    upward = is_upward(me_ref[0], step)
    first_out_ref[...] = jnp.where(upward, sums[0], sums[1])
    second_out_ref[...] = jnp.where(upward, sums[1], sums[0])


def halo_sums(width, step, products, came, me):
    pixels, taps = products[0].shape
    out = jax.ShapeDtypeStruct((pixels, taps // 3), jnp.float32)
    kernel = functools.partial(halo_kernel, width, step)
    return halo_call(kernel, "halo_sums", out, me, *products, came)


def shift_kernel(width, step, flip, me_ref, first_ref, second_ref, first_out_ref, second_out_ref):
    branch = first_ref.shape[1]
    upward = is_upward(me_ref[0] ^ flip, step)
    first, second = first_ref[...].astype(jnp.float32), second_ref[...].astype(jnp.float32)
    pairs = ((first, second, first_out_ref), (second, first, second_out_ref))
    for here, there, out_ref in pairs:
        block = jnp.where(upward, here, there)
        for j in range(3):
            moved = moved_rows(block, width, (1 - j) * DILATION_RATE)
            out_ref[:, j * branch : (j + 1) * branch] = moved.astype(jnp.bfloat16)


def shifted(width, step, first, second, me, flip=0):
    pixels, branch = first.shape
    out = jax.ShapeDtypeStruct((pixels, 3 * branch), jnp.bfloat16)
    kernel = functools.partial(shift_kernel, width, step, flip)
    return halo_call(kernel, "shift", out, me, first, second)


def halo_call(kernel, name, out, me, first, *others):
    return pl.pallas_call(
        kernel,
        out_shape=(out, out),
        in_specs=[pl.BlockSpec(memory_space=pltpu.SMEM)]
        + [pl.BlockSpec(memory_space=pltpu.VMEM)] * (1 + len(others)),
        out_specs=(pl.BlockSpec(memory_space=pltpu.VMEM),) * 2,
        cost_estimate=pl.CostEstimate(
            flops=0, bytes_accessed=8 * (first.size + out.size), transcendentals=0
        ),
        compiler_params=pltpu.CompilerParams(vmem_limit_bytes=8 << 20),
        name=name,
    )(me.reshape(1), first, *others)


def merge_gradient_kernel(me_ref, joined_ref, grad_out_ref, own_ref, other_ref, total_ref):
    me = me_ref[0]
    total_ref[...] = dot_f32(joined_ref[...], grad_out_ref[...], 0, 0)
    half = own_ref.shape[0]
    group = 8
    for k in range(half // group):
        here = slice(k * group, (k + 1) * group)
        device = (2 * k) ^ me
        own_ref[here, :] = total_ref[pl.ds(pl.multiple_of(device * group, group), group), :]
        device = (2 * k + 1) ^ me
        other_ref[here, :] = total_ref[pl.ds(pl.multiple_of(device * group, group), group), :]


def merge_gradient(joined, grad_out, me):
    pixels, width = joined.shape
    half = jax.ShapeDtypeStruct((width // 2, grad_out.shape[1]), jnp.float32)
    return pl.pallas_call(
        merge_gradient_kernel,
        out_shape=(half, half),
        in_specs=[pl.BlockSpec(memory_space=pltpu.SMEM)]
        + [pl.BlockSpec(memory_space=pltpu.VMEM)] * 2,
        out_specs=(pl.BlockSpec(memory_space=pltpu.VMEM),) * 2,
        scratch_shapes=[pltpu.VMEM((width, grad_out.shape[1]), jnp.float32)],
        cost_estimate=pl.CostEstimate(
            flops=2 * pixels * width * grad_out.shape[1],
            bytes_accessed=8 * pixels * width,
            transcendentals=0,
        ),
        compiler_params=pltpu.CompilerParams(vmem_limit_bytes=8 << 20),
        name="merge_gradient",
    )(me.reshape(1), joined, grad_out)


def layout(rows, merge_rows, merge_width):
    shares = (0, rows // 4, 3 * rows // 8, rows)
    tables = []
    for p, portion in enumerate(PORTIONS):
        table = [(k, 0, n * rows, rows) for n, k in enumerate(k for k in portion if k > 0)]
        table.append((0, shares[p], 3 * rows, shares[p + 1] - shares[p]))
        if p == 2:
            first = 3 * rows + table[-1][3]
            lanes = range(0, merge_width, LANES)
            table += [(None, x, first + n * merge_rows, merge_rows) for n, x in enumerate(lanes)]
        tables.append(table)
    return tables


def stack_rows(table):
    return table[-1][2] + table[-1][3]


def lanes_of(k):
    for p, portion in enumerate(PORTIONS):
        if k in portion:
            at = portion.index(k) * LANES
            return p, slice(at, at + LANES)


def local_call(kernel, name, out_shape, operands, moved, grant):
    return pl.pallas_call(
        kernel,
        out_shape=out_shape,
        in_specs=[pl.BlockSpec(memory_space=pltpu.VMEM)] * len(operands),
        out_specs=[pl.BlockSpec(memory_space=pltpu.VMEM)] * len(out_shape),
        cost_estimate=pl.CostEstimate(flops=moved // 4, bytes_accessed=moved, transcendentals=0),
        compiler_params=pltpu.CompilerParams(vmem_limit_bytes=grant << 20),
        name=name,
    )(*operands)


def pack_kernel(tables, weight_ref, merge_ref, out_ref, sems):
    copies, base = [], 0
    for table in tables:
        for k, there, here, count in table:
            if k is None:
                source = merge_ref.at[:, pl.ds(there, LANES)]
            else:
                source = weight_ref.at[k, pl.ds(there, count), :]
            target = out_ref.at[pl.ds(base + here, count), :]
            copies.append(pltpu.make_async_copy(source, target, sems.at[len(copies)]))
        base += stack_rows(table)
    for copy in copies:
        copy.start()
    for copy in copies:
        copy.wait()


def pack(weight, merge_weight, tables):
    return pl.pallas_call(
        functools.partial(pack_kernel, tables),
        out_shape=jax.ShapeDtypeStruct((sum(map(stack_rows, tables)), LANES), weight.dtype),
        in_specs=[pl.BlockSpec(memory_space=pltpu.HBM)] * 2,
        out_specs=pl.BlockSpec(memory_space=pltpu.VMEM),
        scratch_shapes=[pltpu.SemaphoreType.DMA((sum(map(len, tables)),))],
        cost_estimate=pl.CostEstimate(flops=0, bytes_accessed=4 * weight.size, transcendentals=0),
        compiler_params=pltpu.CompilerParams(vmem_limit_bytes=4 << 20),
        name="pack",
    )(*(pltpu.with_memory_space_constraint(x, pltpu.HBM) for x in (weight, merge_weight)))


def block_pair(target, inner):
    low = target // inner * (2 * inner) + target % inner
    return low, low + inner


def unpack_kernel(tables, inners, *refs):
    outs = refs[6:]

    def step(target, carry):
        for p, table in enumerate(tables):
            for ref, block in zip(refs[2 * p : 2 * p + 2], block_pair(target, inners[p])):
                for k, there, here, count in table:
                    value = ref[target, here : here + count, :]
                    if k is None:
                        outs[3][block, :, there : there + LANES] = value
                    else:
                        q, lanes = lanes_of(k)
                        outs[q][block, there : there + count, lanes] = value
        return carry

    lax.fori_loop(0, refs[0].shape[0], step, 0)


def unpack(pairs, tables, inners, rows, merge_rows, merge_width):
    blocks = 2 * pairs[0].shape[0]
    shapes = [(blocks, rows, LANES * len(p)) for p in PORTIONS] + [(blocks, merge_rows, merge_width)]
    out = [jax.ShapeDtypeStruct(x, jnp.bfloat16) for x in shapes]
    kernel = functools.partial(unpack_kernel, tables, tuple(inners))
    return local_call(kernel, "unpack", out, pairs, 4 * sum(x.size for x in pairs), 16)


def first_fold_kernel(tables, inners, *refs):
    owns, arrived, keeps, sends = refs[:4], refs[4], refs[5:8], refs[8:]

    def step(target, carry):
        for p, table in enumerate(tables):
            for half, block in enumerate(block_pair(target, inners[p])):
                for k, there, here, count in table:
                    if k is None:
                        q, at = 3, (block, slice(None), slice(there, there + LANES))
                    else:
                        q, lanes = lanes_of(k)
                        at = (block, slice(there, there + count), lanes)
                    value = owns[q][at]
                    if k is None:
                        value = value + arrived[at]
                    out_ref = (keeps, sends)[half][p]
                    out_ref[target, here : here + count, :] = value.astype(out_ref.dtype)
        return carry

    lax.fori_loop(0, keeps[0].shape[0], step, 0)


def fold_kernel(inners, *refs):
    owns, arriveds, keeps, sends = (refs[3 * k : 3 * k + 3] for k in range(4))

    def step(target, carry):
        for p in range(3):
            for half, block in enumerate(block_pair(target, inners[p])):
                value = owns[p][block] + arriveds[p][block].astype(jnp.float32)
                out_ref = (keeps, sends)[half][p]
                out_ref[target] = value.astype(out_ref.dtype)
        return carry

    lax.fori_loop(0, keeps[0].shape[0], step, 0)


def fold(owns, arriveds, tables, inners):
    shapes = [(owns[0].shape[0] // 2, stack_rows(table), LANES) for table in tables]
    out = [jax.ShapeDtypeStruct(x, t) for t in (jnp.float32, jnp.bfloat16) for x in shapes]
    if len(owns) == 4:
        kernel = functools.partial(first_fold_kernel, tables, tuple(inners))
    else:
        kernel = functools.partial(fold_kernel, tuple(inners))
    moved = 9 * sum(x.size for x in owns)
    out = local_call(kernel, "fold", out, (*owns, *arriveds), moved, 20)
    return out[:3], out[3:]


def last_fold_kernel(*refs):
    owns, arriveds = refs[:3], refs[3:6]
    base = 0
    for own, arrived in zip(owns, arriveds):
        at = slice(base, base + own.shape[1])
        base += own.shape[1]
        refs[6][at, :] = own[0] + arrived[0].astype(jnp.float32)
        refs[7][at, :] = (own[1] + arrived[1].astype(jnp.float32)).astype(jnp.bfloat16)


def last_fold(owns, arriveds):
    shape = (sum(x.shape[1] for x in owns), LANES)
    out = [jax.ShapeDtypeStruct(shape, t) for t in (jnp.float32, jnp.bfloat16)]
    moved = 9 * sum(x.size for x in owns)
    return local_call(last_fold_kernel, "last_fold", out, (*owns, *arriveds), moved, 8)


def scaled_kernel(tables, scale, keep_ref, arrived_ref, out_ref, out_merge_ref):
    base = 0
    for table in tables:
        for k, there, here, count in table:
            at = slice(base + here, base + here + count)
            value = (keep_ref[at, :] + arrived_ref[at, :].astype(jnp.float32)) * scale
            if k is None:
                out_merge_ref[:, there : there + LANES] = value
            else:
                out_ref[k, there : there + count, :] = value
        base += stack_rows(table)


def scaled(keep, arrived, tables, scale, rows, merge_rows, merge_width):
    taps = sum(map(len, PORTIONS))
    out = [
        jax.ShapeDtypeStruct((taps, rows, LANES), jnp.float32),
        jax.ShapeDtypeStruct((merge_rows, merge_width), jnp.float32),
    ]
    kernel = functools.partial(scaled_kernel, tables, scale)
    return local_call(kernel, "scaled", out, (keep, arrived), 10 * keep.size, 8)


def column_shifted(rows, shift):
    width = rows.shape[1]
    if shift == 0:
        return rows
    if shift > 0:
        return jnp.pad(rows[:, shift:], ((0, 0), (0, shift), (0, 0)))
    return jnp.pad(rows[:, : width + shift], ((0, 0), (-shift, 0), (0, 0)))


def on_device(
    features, branch_kernel_weight, branch_norm_bias, merge_weight, merge_bias, cotangent
):
    device_count = lax.axis_size("row")
    bit_count = device_count.bit_length() - 1
    me = lax.axis_index("row")
    rows, width, channels = features.shape
    taps, branch = branch_kernel_weight.shape[1:]
    own_channels = branch_kernel_weight.shape[0]
    joined_rows, merged_width = merge_weight.shape
    joined_width = joined_rows * device_count
    pixels = rows * width
    scale = 1.0 / math.sqrt(rows * device_count * width)
    device_step = DILATION_RATE // rows
    bits = (1,) * (bit_count - 1)
    orders = bit_orders(bit_count)
    far_bits = list(range(bit_count - 1, 3, -1))
    paired = 2 * own_channels == LANES and joined_rows == 8 and branch == LANES and bit_count == 5
    portion_widths = [len(p) * branch for p in PORTIONS]

    def split(array, widths):
        starts = [sum(widths[:i]) for i in range(len(widths))]
        return [lax.slice_in_dim(array, s, s + w, axis=-1) for s, w in zip(starts, widths)]

    tap_order = [k for portion in PORTIONS for k in portion]
    weight = branch_kernel_weight.transpose(1, 0, 2)
    half_rows = channels // 2
    crossing = orders + [orders[1]]
    flat = features.reshape(pixels, channels)
    if paired:
        tables = layout(own_channels, joined_rows, merged_width)
        block = pack(weight, merge_weight, tables)
        block, flat, me = together(block, flat, me)
        flat_own, flat_other = reordered(flat, me)
        block = block.reshape(bits + block.shape)
        (arrived,) = together(exchanged(block, far_bits[0]))
        block, arrived, flat_own, flat_other = together(block, arrived, flat_own, flat_other)
        blocks, base = [], 0
        for table in tables:
            parts = [
                lax.slice_in_dim(x, base, base + stack_rows(table), axis=-2) for x in (block, arrived)
            ]
            blocks.append(jnp.concatenate(parts, axis=0))
            base += stack_rows(table)
        for step in range(len(orders[0]) - 1):
            blocks = gathered(together(*blocks), [o[step] for o in orders], bit_count)
        *blocks, flat_partner = together(*blocks, exchanged(flat_other, 0))
        arrived = together(*[exchanged(b, o[-1]) for b, o in zip(blocks, orders)])
        pairs = [
            x.reshape((device_count // 4,) + x.shape[-2:])
            for pair in zip(blocks, arrived)
            for x in pair
        ]
        inners = [1 << (o[-1] - 1) for o in orders]
        *own_weight, own_merge = unpack(
            pairs, tables, inners, own_channels, joined_rows, merged_width
        )
        own_weight = [x.reshape(half_rows, x.shape[-1]) for x in own_weight]
    else:
        block = jnp.concatenate([weight[k] for k in tap_order], axis=1)
        to_relative = relative_order(channels, device_count, me)
        flat = dot_f32(flat, to_relative, 1, 0).astype(jnp.bfloat16)
        flat_own, flat_other = flat[:, :half_rows], flat[:, half_rows:]
        block = block.reshape(bits + block.shape)
        merge_block = merge_weight.reshape(bits + merge_weight.shape)
        for bit in far_bits:
            block, merge_block = gathered([block, merge_block], [bit, bit], bit_count)
        blocks = split(block, portion_widths) + [merge_block]
        for step in range(len(orders[0])):
            blocks = gathered(together(*blocks), [o[step] for o in crossing], bit_count)
        own_merge = blocks.pop()
        own_weight = [b.reshape(half_rows, b.shape[-1]) for b in blocks]
    own_merge = own_merge.reshape(joined_width // 2, merged_width)

    def row_sum(parts):
        total = None
        for j, part in enumerate(parts):
            moved = column_shifted(part.reshape(rows, width, branch), (j - 1) * DILATION_RATE)
            total = moved if total is None else total + moved
        return total

    def by_tap(product):
        return split(product, [branch] * (product.shape[1] // branch))

    upward = is_upward(me, device_step)
    if paired:
        sums = partner_sums(width, [dot_f32(flat_partner, w, 1, 0) for w in own_weight[:2]])
        sums, own_weight[0], own_weight[1] = together(sums, *own_weight[:2])
        products = [dot_f32(flat_own, w, 1, 0) for w in own_weight[:2]]
        came, *products = together(exchanged(sums, 0), *products)
        sums = halo_sums(width, device_step, products, came, me)
        other_weight = [None, None]
    else:
        other_weight = [exchanged(w, 0) for w in own_weight[:2]]
        sums = [
            dot_f32(flat_own, a, 1, 0) + dot_f32(flat_other, b, 1, 0)
            for a, b in zip(own_weight, other_weight)
        ]
        sums = [row_sum(by_tap(x)).reshape(pixels, branch) for x in sums]
        sums = [jnp.where(upward, *sums), jnp.where(upward, *sums[::-1])]
    merge_to_relative = relative_order(joined_width, device_count, me)
    own_weight[2], own_merge, *sums = together(own_weight[2], own_merge, *sums)
    whole_merge = dot_f32(
        merge_to_relative, jnp.concatenate([own_merge, exchanged(own_merge, 0)], axis=0), 1, 0
    ).astype(jnp.bfloat16)
    other_weight.append(exchanged(own_weight[2], 0))
    centre = dot_f32(flat_own, own_weight[2], 1, 0) + dot_f32(flat_other, other_weight[2], 1, 0)
    above, below = swapped(sums[0], device_step, 0), swapped(sums[1], device_step, 1)
    flat_cotangent = cotangent.reshape(pixels, merged_width)
    if paired:
        merged, grad_dil, centre_gradient, joined, grad_out = head(
            width, centre, above, below, branch_norm_bias, whole_merge, merge_bias, flat_cotangent
        )
    else:
        centre = by_tap(centre)
        z_dil = row_sum(centre[1:]).reshape(pixels, branch) + above + below
        act_one = jnp.maximum(centre[0] + branch_norm_bias[0], 0.0).astype(jnp.bfloat16)
        act_dil = jnp.maximum(z_dil + branch_norm_bias[1], 0.0).astype(jnp.bfloat16)
        joined = jnp.concatenate([act_one, act_dil], axis=1)
        merged = jnp.maximum(dot_f32(joined, whole_merge, 1, 0) + merge_bias, 0.0)
        merged = merged.astype(jnp.bfloat16)
        grad_out = jnp.where(merged > 0, flat_cotangent, jnp.zeros((), jnp.bfloat16))
        back = dot_f32(grad_out, whole_merge, 1, 1)
        kept = jnp.where(joined > 0, back, 0.0).astype(jnp.bfloat16)
        grad_dil = kept[:, branch:]
        centre_gradient = None

    def shifted_gradients(block):
        block = block.reshape(rows, width, branch)
        parts = [column_shifted(block, (1 - j) * DILATION_RATE) for j in range(3)]
        return [part.reshape(pixels, branch) for part in parts]

    if not paired:
        centre_gradient = jnp.concatenate([kept[:, :branch]] + shifted_gradients(grad_dil), axis=1)
    halos = [swapped(grad_dil, device_step, 0), swapped(grad_dil, device_step, 1)]
    if paired:
        own_merge, other_merge = merge_gradient(joined, grad_out, me)
    else:
        joined_relative = dot_f32(joined, merge_to_relative, 1, 0).astype(jnp.bfloat16)
        merge_total = dot_f32(joined_relative, grad_out, 0, 0)
        own_merge = merge_total[: joined_width // 2]
        other_merge = merge_total[joined_width // 2 :]
    merge_arrived = exchanged(other_merge, 0)

    centre_gradient, own_merge = together(centre_gradient, own_merge)
    own_total, other_total = [None] * 3, [None] * 3
    own_total[2] = dot_f32(flat_own, centre_gradient, 0, 0)
    if paired:
        partner_gradient = exchanged(centre_gradient, 0)
        own_total[2] = own_total[2] + dot_f32(flat_partner, partner_gradient, 0, 0)
        other_weight[:2] = [exchanged(w, 0) for w in own_weight[:2]]
        *halos, own_total[2], other_weight[0], other_weight[1] = together(
            *halos, own_total[2], *other_weight[:2]
        )
        partner_halos = [exchanged(h, 0) for h in halos]
        gradients = [*shifted(width, device_step, *halos, me), centre_gradient]
        own_total[:2] = [dot_f32(flat_own, g, 0, 0) for g in gradients[:2]]
        *partner_halos, own_total[0], own_total[1] = together(*partner_halos, *own_total[:2])
        partner_gradients = shifted(width, device_step, *partner_halos, me, 1)
        for p in range(2):
            own_total[p] = own_total[p] + dot_f32(flat_partner, partner_gradients[p], 0, 0)
    else:
        other_total[2] = dot_f32(flat_other, centre_gradient, 0, 0).astype(jnp.bfloat16)
        *halos, own_total[2], other_total[2] = together(*halos, own_total[2], other_total[2])
        halos = [jnp.where(upward, *halos), jnp.where(upward, *halos[::-1])]
        gradients = [jnp.concatenate(shifted_gradients(h), axis=1) for h in halos]
        gradients = together(*gradients) + [centre_gradient]
        for p in range(2):
            other_total[p] = dot_f32(flat_other, gradients[p], 0, 0).astype(jnp.bfloat16)
            own_total[p] = dot_f32(flat_own, gradients[p], 0, 0)
    if paired:
        own_blocks = device_count // 2
        owns = [x.reshape(own_blocks, -1, x.shape[-1]) for x in (*own_total, own_merge)]
        arrived = [merge_arrived.reshape(owns[3].shape)]
        left = [list(range(bit_count - 1, 0, -1)) for _ in orders]
        for step in range(len(orders[0])):
            bits_now = [o[-1 - step] for o in orders]
            inners = [1 << (len(x) - 1 - x.index(b)) for x, b in zip(left, bits_now)]
            owns, sent = fold(owns, arrived, tables, inners)
            for x, b in zip(left, bits_now):
                x.remove(b)
            if step == 0:
                *sent, g0, g1, g2 = together(*sent, *gradients)
                input_grad, merged = input_gradient(
                    [g0, g1, g2], own_weight, other_weight, me, merged
                )
            else:
                sent = together(*sent)
            arrived = together(*[exchanged(t, b) for t, b in zip(sent, bits_now)])
            if step == 0:
                *arrived, input_grad = together(*arrived, input_grad)
        keep, sent = last_fold(owns, arrived)
        branch_kernel_gradient, grad_merge = scaled(
            keep,
            exchanged(sent, far_bits[0]),
            tables,
            scale,
            own_channels,
            joined_rows,
            merged_width,
        )
        branch_kernel_gradient = branch_kernel_gradient.transpose(1, 0, 2)
    else:
        merge_total = own_merge + merge_arrived.astype(jnp.float32)
        merge_total = merge_total.reshape((2,) * (bit_count - 1) + (joined_rows, merged_width))
        merge_parts = halves(merge_total, far_bits[0], bit_count) if far_bits else None
        sending = list(other_total) + ([merge_parts[1]] if far_bits else [])
        arrived = [
            exchanged(t, b) for t, b in zip(together(*sending), [0, 0, 0] + far_bits[:1])
        ]
        arrived = together(*arrived)
        if far_bits:
            merge_total = merge_parts[0] + arrived.pop().astype(jnp.float32)
        for bit in far_bits[1:]:
            own, other = halves(merge_total, bit, bit_count)
            merge_total = own + exchanged(other, bit).astype(jnp.float32)
        totals = []
        for own, a, o in zip(own_total, arrived, orders):
            shape = (2,) * (bit_count - 1) + (own.shape[0] // (device_count // 2), own.shape[1])
            totals.append(added(own.reshape(shape), a.reshape(shape), o[-1], bit_count))
        totals.append(halves(merge_total, crossing[3][-1], bit_count))
        *sent, g0, g1, g2 = together(*[t[1] for t in totals], *gradients)
        input_total = sum(
            dot_f32(g, jnp.concatenate([a, b], axis=0), 1, 1)
            for g, a, b in zip((g0, g1, g2), own_weight, other_weight)
        ).astype(jnp.bfloat16)
        input_grad = dot_f32(input_total, to_relative, 1, 1).astype(jnp.bfloat16)
        for step in range(len(orders[0])):
            arrived = together(*[exchanged(t, o[-1 - step]) for t, o in zip(sent, crossing)])
            if step == 0:
                *arrived, input_grad = together(*arrived, input_grad)
            own = [t[0] for t in totals]
            if step + 1 < len(orders[0]):
                totals = [
                    added(t, a, o[-2 - step], bit_count) for t, a, o in zip(own, arrived, crossing)
                ]
                sent = together(*[t[1] for t in totals])
            else:
                totals = [t + a.astype(jnp.float32) for t, a in zip(own, arrived)]
        grad_merge = totals[3].reshape(joined_rows, merged_width) * scale
        total = jnp.concatenate(totals[:3], axis=-1)
        for bit in far_bits[::-1]:
            own, other = halves(total, bit, bit_count)
            total = own + exchanged(other, bit).astype(jnp.float32)
        weight_gradient = dict(
            zip([k for p in PORTIONS for k in p], by_tap(total.reshape(own_channels, -1)))
        )
        branch_kernel_gradient = jnp.stack([weight_gradient[k] for k in range(taps)], axis=1) * scale

    return (
        merged.reshape(rows, width, merged_width),
        input_grad.reshape(rows, width, channels),
        branch_kernel_gradient,
        grad_merge,
    )


def solution(mesh):
    placed = (
        P(("grp", "row"), None, None),
        P("row", None, None),
        P(),
        P("row", None),
        P(),
        P(("grp", "row"), None, None),
    )
    return jax.shard_map(
        on_device,
        mesh=mesh,
        in_specs=placed,
        out_specs=(
            P(("grp", "row"), None, None),
            P(("grp", "row"), None, None),
            P(("grp", "row"), None, None),
            P(("grp", "row"), None),
        ),
        check_vma=False,
    )
```
